32 devices in a mesh: groups: 2 (over y), wide: 4 (over z), narrow: 4 (over x, core).
Axes of the slice: x: 2, y: 2, z: 4, core: 2. Of those that a mesh axis runs over, the one named last changes fastest.
Arguments:
- populations: float32 [19, 96, 192, 128], P(None, ('groups', 'wide'), 'narrow'), parts along dimension 1, may hold values from 0.008 to 0.57, as said below
- flags: int32 [96, 192, 128], P(('groups', 'wide'), 'narrow'), parts along dimension 0, may hold values from 0 to 3, as said below
- potential: float32 [24, 48, 32], P(('groups', 'wide'), 'narrow'), parts along dimension 0, may hold values from -6 to 6
- conductivity: float32 [24, 48, 32], P(('groups', 'wide'), 'narrow'), parts along dimension 0, may hold values from 0.5 to 2
- coil_phase: int32 [24, 48, 32], P(('groups', 'wide'), 'narrow'), parts along dimension 0, may hold values from 0 to 2
- phase_table: float32 [3, 4], replicated, may hold values from -4 to 4
- magnetic: float32 [3, 24, 48, 32], P(None, ('groups', 'wide'), 'narrow'), parts along dimension 1, may hold values from -6 to 6
Outputs:
- populations_out: float32 [19, 96, 192, 128], P(None, ('groups', 'wide'), 'narrow'), parts along dimension 1
- potential_out: float32 [24, 48, 32], P(('groups', 'wide'), 'narrow'), parts along dimension 0
- lorentz: float32 [3, 24, 48, 32], P(None, ('groups', 'wide'), 'narrow'), parts along dimension 1
The draws below stay inside these ranges and needn't reach their ends.
There are 2 independent parts, one for each index of `groups`. The reference program is written for one: setup_inputs(seed, part) draws one part's arguments, and reference() takes and returns one part's arrays. A program takes and returns all parts, laid end to end along the dimension named above; an argument that names none is the same for every part. Nothing has to cross between parts.
Inputs may be any that keep to these rules, and one draw needn't show every extreme that they name: flags: 0 fluid, 1 wall, 2 inlet, 3 outlet. `populations`: each population is its lattice weight times a positive factor.
All inputs are finite; a program needn't handle non-finite values.
Results may differ from the reference program's by a relative error of at most 0.00002.
Values sent between devices are 32-bit elements; how exact they have to be, the bound alone decides.
No kernel may reach another device: no remote copies, remote signals or barrier semaphores. Data moves between devices by JAX's collectives and lax.ppermute only.
A program may use at most 64 MiB of HBM per device.

```python
import math
import jax
import jax.numpy as jnp

FX = 128
Q = 19
SWEEPS = 2
NY = 192
NZ = 48
KX = 32
KY = 48
KZ = 12


lattice_weights = [1.0 / 3.0] + [1.0 / 18.0] * 6 + [1.0 / 36.0] * 12


def draw_populations(key, part):
    weights = jnp.array(lattice_weights, jnp.float32)[:, None, None, None]
    factor = jax.random.uniform(key, (Q, NZ, NY, FX), jnp.float32, 0.5, 1.5)
    return weights * factor


def draw_flags(key, part):
    rolled = jax.random.randint(key, (NZ, NY, FX), 0, 20)
    return jnp.where(rolled < 16, 0, jnp.where(rolled < 18, 1, jnp.where(rolled < 19, 2, 3))).astype(jnp.int32)


def touch_ends(entries, stream_key, low, largest):
    spot = [jax.random.randint(jax.random.fold_in(stream_key, axis), (), 0, length) for axis, length in enumerate(entries.shape)]
    longest = entries.shape.index(max(entries.shape))
    beside = spot[:longest] + [(spot[longest] + 1) % entries.shape[longest]] + spot[longest + 1:]
    return entries.at[tuple(spot)].set(low).at[tuple(beside)].set(largest)


def steps_of(stream_key, extent, pieces, low, top_value):
    def one(axis_at, parts):
        heights = jax.random.uniform(jax.random.fold_in(jax.random.fold_in(stream_key, 6), axis_at), (parts,), jnp.float32, low / len(pieces), top_value / len(pieces))
        return jnp.repeat(jnp.exp(heights), extent[axis_at] // parts).reshape((-1,) + (1,) * (len(extent) - axis_at - 1))

    gain = one(*pieces[0])
    for cut in pieces[1:]:
        gain = gain * one(*cut)
    return gain


def gaussian(own_key, dims, width, reach, shards=(), kind=jnp.bfloat16):
    entries = jax.random.normal(own_key, dims, jnp.float32) * width
    if len(shards) > 0:
        entries = steps_of(own_key, dims, shards, -0.22, 0.18) * entries
    return jnp.clip(entries, min=-reach, max=reach).astype(kind)


def setup_inputs(seed: int = 0, part: int = 0) -> dict:
    key_list = jax.random.split(jax.random.key(seed), 8)
    own_keys = jax.random.split(jax.random.fold_in(key_list[7], part), 8)
    return {
        "populations": draw_populations(jax.random.fold_in(jax.random.fold_in(key_list[7], part), 71), part),
        "flags": draw_flags(jax.random.fold_in(jax.random.fold_in(key_list[7], part), 71), part),
        "potential": gaussian(own_keys[2], (KZ, KY, KX), 1.0, 6.0, ((0, 4), (1, 4)), jnp.float32),
        "conductivity": jnp.clip(jnp.exp(math.log(2.0) - 1.3862944 * jax.random.uniform(own_keys[3], (KZ, KY, KX), jnp.float32) ** steps_of(own_keys[3], (KZ, KY, KX), ((0, 4), (1, 4)), -0.2, 0.2)), 0.5, 2.0),
        "coil_phase": touch_ends(jax.random.randint(own_keys[4], (KZ, KY, KX), 0, 3), jax.random.fold_in(own_keys[4], 1), 0, 2).astype(jnp.int32),
        "phase_table": gaussian(key_list[5], (3, 4), 1.0, 4.0, (), jnp.float32),
        "magnetic": gaussian(own_keys[6], (3, KZ, KY, KX), 1.0, 6.0, ((1, 4), (2, 4)), jnp.float32),
    }


lattice_dirs = [(0, 0, 0), (1, 0, 0), (-1, 0, 0), (0, 1, 0), (0, -1, 0), (0, 0, 1), (0, 0, -1), (1, 1, 0), (-1, -1, 0), (1, -1, 0), (-1, 1, 0), (1, 0, 1), (-1, 0, -1), (1, 0, -1), (-1, 0, 1), (0, 1, 1), (0, -1, -1), (0, 1, -1), (0, -1, 1)]
opposite_dir = [0, 2, 1, 4, 3, 6, 5, 8, 7, 10, 9, 12, 11, 14, 13, 16, 15, 18, 17]
lattice_weights = [1.0 / 3.0] + [1.0 / 18.0] * 6 + [1.0 / 36.0] * 12
relax_time = 0.8
force_scale = 0.02
inlet_speed = 0.05


def phase_lookup(coil_phase, phase_table, column):
    summed = jnp.zeros(coil_phase.shape, jnp.float32)
    for phase in range(3):
        summed = summed + jnp.where(coil_phase == phase, phase_table[phase, column], jnp.float32(0.0))
    return summed


def jacobi_sweep(padded, source):
    beside_all = padded[2:, 1:-1, 1:-1] + padded[:-2, 1:-1, 1:-1]
    beside_all = beside_all + padded[1:-1, 2:, 1:-1] + padded[1:-1, :-2, 1:-1]
    beside_all = beside_all + padded[1:-1, 1:-1, 2:] + padded[1:-1, 1:-1, :-2]
    return (beside_all + source) / 6.0


def gradients(padded):
    grad_z = (padded[2:, 1:-1, 1:-1] - padded[:-2, 1:-1, 1:-1]) * 0.5
    grad_y = (padded[1:-1, 2:, 1:-1] - padded[1:-1, :-2, 1:-1]) * 0.5
    grad_x = (padded[1:-1, 1:-1, 2:] - padded[1:-1, 1:-1, :-2]) * 0.5
    return grad_x, grad_y, grad_z


def lorentz_from(grad_x, grad_y, grad_z, conductivity, coil_phase, phase_table, magnetic):
    cur_x = conductivity * (phase_lookup(coil_phase, phase_table, 1) - grad_x)
    cur_y = conductivity * (phase_lookup(coil_phase, phase_table, 2) - grad_y)
    cur_z = conductivity * (phase_lookup(coil_phase, phase_table, 3) - grad_z)
    field_x, field_y, field_z = magnetic[0], magnetic[1], magnetic[2]
    return jnp.stack([cur_y * field_z - cur_z * field_y, cur_z * field_x - cur_x * field_z, cur_x * field_y - cur_y * field_x])


def upsample(lorentz):
    grown = jnp.repeat(jnp.repeat(jnp.repeat(lorentz, 4, axis=1), 4, axis=2), 4, axis=3)
    return grown * force_scale


def collide(popul, flags, force):
    density = jnp.sum(popul, axis=0)
    force_x, force_y, force_z = force[0], force[1], force[2]
    mom_x = jnp.zeros_like(density)
    mom_y = jnp.zeros_like(density)
    mom_z = jnp.zeros_like(density)
    for number in range(19):
        step_x, step_y, step_z = lattice_dirs[number]
        if step_x != 0:
            mom_x = mom_x + step_x * popul[number]
        if step_y != 0:
            mom_y = mom_y + step_y * popul[number]
        if step_z != 0:
            mom_z = mom_z + step_z * popul[number]
    vel_x = (mom_x + 0.5 * force_x) / density
    vel_y = (mom_y + 0.5 * force_y) / density
    vel_z = (mom_z + 0.5 * force_z) / density
    speed_sq = vel_x * vel_x + vel_y * vel_y + vel_z * vel_z
    factor = 1.0 - 0.5 / relax_time
    merged = []
    for number in range(19):
        step_x, step_y, step_z = lattice_dirs[number]
        weight = lattice_weights[number]
        along_u = step_x * vel_x + step_y * vel_y + step_z * vel_z
        along_f = step_x * force_x + step_y * force_y + step_z * force_z
        shape_eq = 1.0 + 3.0 * along_u + 4.5 * along_u * along_u - 1.5 * speed_sq
        balanced = weight * density * shape_eq
        forcing = factor * weight * (3.0 * ((step_x - vel_x) * force_x + (step_y - vel_y) * force_y + (step_z - vel_z) * force_z) + 9.0 * along_u * along_f)
        relaxed = popul[number] - (popul[number] - balanced) / relax_time + forcing
        outflow = weight * shape_eq
        along_in = -step_z * inlet_speed
        inflow = jnp.full_like(density, weight * (1.0 + 3.0 * along_in + 4.5 * along_in * along_in - 1.5 * inlet_speed * inlet_speed))
        chosen = jnp.where(flags == 0, relaxed, jnp.where(flags == 2, inflow, jnp.where(flags == 3, outflow, popul[number])))
        merged.append(chosen)
    return jnp.stack(merged)


def bounce_back(post, pulled, open_pad, flags):
    size_z, size_y, size_x = flags.shape
    merged = []
    for number in range(19):
        step_x, step_y, step_z = lattice_dirs[number]
        open_src = open_pad[1 - step_z:1 - step_z + size_z, 1 - step_y:1 - step_y + size_y, 1 - step_x:1 - step_x + size_x]
        read = jnp.where(open_src == 1, pulled[number], post[opposite_dir[number]])
        merged.append(jnp.where(flags == 1, post[number], read))
    return jnp.stack(merged)


def pull_padded(post_pad, shape):
    size_z, size_y, size_x = shape
    pulled = []
    for number in range(19):
        step_x, step_y, step_z = lattice_dirs[number]
        pulled.append(post_pad[number, 1 - step_z:1 - step_z + size_z, 1 - step_y:1 - step_y + size_y, 1 - step_x:1 - step_x + size_x])
    return pulled


def reference(populations, flags, potential, conductivity, coil_phase, phase_table, magnetic):
    source = conductivity * phase_lookup(coil_phase, phase_table, 0)
    potential_now = potential
    for counter in range(SWEEPS):
        potential_now = jacobi_sweep(jnp.pad(potential_now, 1), source)
    grad_x, grad_y, grad_z = gradients(jnp.pad(potential_now, 1))
    lorentz = lorentz_from(grad_x, grad_y, grad_z, conductivity, coil_phase, phase_table, magnetic)
    force = upsample(lorentz)
    post = collide(populations, flags, force)
    open_cells = (flags != 1).astype(jnp.int32)
    open_pad = jnp.pad(open_cells, 1)
    post_pad = jnp.pad(post, ((0, 0), (1, 1), (1, 1), (1, 1)))
    pulled = pull_padded(post_pad, flags.shape)
    result = bounce_back(post, pulled, open_pad, flags)
    return result, potential_now, lorentz
```

```python
import jax
import jax.numpy as jnp
from jax import lax
from jax.experimental import pallas as pl
from jax.experimental.pallas import tpu as pltpu
from jax.sharding import PartitionSpec as P

lattice_dirs = [
    (0, 0, 0),
    (1, 0, 0),
    (-1, 0, 0),
    (0, 1, 0),
    (0, -1, 0),
    (0, 0, 1),
    (0, 0, -1),
    (1, 1, 0),
    (-1, -1, 0),
    (1, -1, 0),
    (-1, 1, 0),
    (1, 0, 1),
    (-1, 0, -1),
    (1, 0, -1),
    (-1, 0, 1),
    (0, 1, 1),
    (0, -1, -1),
    (0, 1, -1),
    (0, -1, 1),
]
opposite_dir = [0, 2, 1, 4, 3, 6, 5, 8, 7, 10, 9, 12, 11, 14, 13, 16, 15, 18, 17]
pairs = [(i, opposite_dir[i]) for i in range(1, 19) if i < opposite_dir[i]]
relax_time = 0.8
force_scale = 0.02
inlet_speed = 0.05
force_factor = 1.0 - 0.5 / relax_time

leave_yp = [3, 7, 10, 15, 17]
leave_ym = [4, 8, 9, 16, 18]
leave_zp = [5, 11, 14, 15, 18]
leave_zm = [6, 12, 13, 16, 17]

FACE = 10
GROUPS = 7
POT, SRC, COND, PH, MX, MY, MZ = range(GROUPS)
RIM = 4
CLOSED = -1e30
OPEN_ABOVE = -1e29
VMEM_LIMIT = 48 * 1024 * 1024

any_spec = pl.BlockSpec(memory_space=pl.ANY)
hbm_spec = pl.BlockSpec(memory_space=pltpu.HBM)
vmem_spec = pl.BlockSpec(memory_space=pltpu.VMEM)


def moments(f):
    d = {}
    rho = f[0]
    for i, j in pairs:
        rho = rho + (f[i] + f[j])
        d[i] = f[i] - f[j]
    mx = d[1] + d[7] + d[9] + d[11] + d[13]
    my = d[3] + d[7] - d[9] + d[15] + d[17]
    mz = d[5] + d[11] - d[13] + d[15] - d[17]
    return rho, mx, my, mz


def coefficients(rho, mom, force, fluid, inlet):
    inv = 1.0 / rho
    u = [(m + 0.5 * f) * inv for m, f in zip(mom, force)]
    u = [jnp.where(inlet, c, v) for c, v in zip((0.0, 0.0, -inlet_speed), u)]
    r = jnp.where(fluid, rho * (1.0 / (36.0 * relax_time)), 1.0 / 36.0)
    f = [jnp.where(fluid, v * (force_factor / 36.0), 0.0) for v in force]
    sq = u[0] * u[0] + u[1] * u[1] + u[2] * u[2]
    uf = u[0] * f[0] + u[1] * f[1] + u[2] * f[2]
    base = r * (1.0 - 1.5 * sq) - 3.0 * uf
    ru = [r * v for v in u]
    g = [4.5 * a + 9.0 * b for a, b in zip(ru, f)]
    h = [3.0 * (a + b) for a, b in zip(ru, f)]
    keep = jnp.where(fluid, 1.0 - 1.0 / relax_time, 0.0)
    return keep, base, u, g, h


def along(c, v):
    total = None
    for s, x in zip(c, v):
        if s == 0:
            continue
        if total is None:
            total = x if s > 0 else -x
        else:
            total = total + x if s > 0 else total - x
    return total


def post_pair(i, co):
    keep, base, u, g, h = co
    c = lattice_dirs[i]
    sym = base + along(c, u) * along(c, g)
    anti = along(c, h)
    if sum(abs(s) for s in c) == 1:
        return 2.0 * sym, 2.0 * anti
    return sym, anti


def post_one(i, f, co):
    keep = co[0]
    if i < opposite_dir[i]:
        sym, anti = post_pair(i, co)
        return keep * f + (sym + anti)
    sym, anti = post_pair(opposite_dir[i], co)
    return keep * f + (sym - anti)


def pick(cond, a, b):
    return jnp.where(cond, a, b)


def lanes_to(x, shift):
    shift = shift % 128
    return x if shift == 0 else pltpu.roll(x, shift, 1)


def pack_faces(
    pops,
    flags,
    pot_hbm,
    cond_hbm,
    ph_hbm,
    mag_hbm,
    tab_hbm,
    o_z1,
    o_z2,
    o_y1,
    o_y2,
    o_g,
    pbuf,
    ybuf,
    fpbuf,
    fybuf,
    zsc,
    ysc,
    pot,
    cond,
    ph,
    mag,
    tab,
    sems,
):
    nz, ny = pops.shape[1], pops.shape[2]
    kz, ky, kx = pot.shape
    coarse = [
        pltpu.make_async_copy(a, b, sems.at[8 + k])
        for k, (a, b) in enumerate(
            ((tab_hbm, tab), (ph_hbm, ph), (cond_hbm, cond), (pot_hbm, pot), (mag_hbm, mag))
        )
    ]
    copies = []
    for side, row in ((0, 0), (1, ny - 8)):
        copies.append(
            pltpu.make_async_copy(pops.at[:, :, pl.ds(row, 8), :], ybuf.at[side], sems.at[side])
        )
        copies.append(
            pltpu.make_async_copy(flags.at[:, pl.ds(row, 8), :], fybuf.at[side], sems.at[2 + side])
        )
    for side, plane in ((0, 0), (1, nz - 1)):
        copies.append(pltpu.make_async_copy(pops.at[:, plane], pbuf.at[side], sems.at[4 + side]))
        copies.append(pltpu.make_async_copy(flags.at[plane], fpbuf.at[side], sems.at[6 + side]))
    for c in coarse + copies:
        c.start()
    for c in coarse:
        c.wait()
    phase = ph[...]
    conductivity = cond[...]
    source = conductivity * jnp.where(
        phase == 0, tab[0, 0], jnp.where(phase == 1, tab[1, 0], tab[2, 0])
    )
    fields = [pot[...], source, conductivity, phase.astype(jnp.float32), mag[0], mag[1], mag[2]]
    blank = jnp.zeros((ky, 128 - kz * kx), jnp.float32)
    for g, field in enumerate(fields):
        row = jnp.concatenate([field[l] for l in range(kz)] + [blank], axis=1)
        o_g[g, 0:ky, :] = row
        at = FACE * nz + RIM * g
        ysc[0, at : at + RIM, :] = row[0:RIM]
        ysc[1, at : at + RIM, :] = row[ky - RIM : ky]
    for c in copies[:4]:
        c.wait()
    for side, leave, row in ((0, leave_ym, 0), (1, leave_yp, 7)):
        for z in range(nz):
            f = [ybuf[side, i, z] for i in range(19)]
            values = [f[i] for i in leave] + list(moments(f))
            values.append(fybuf[side, z].astype(jnp.float32))
            for k, v in enumerate(values):
                ysc[side, k * nz + z : k * nz + z + 1, :] = v[row : row + 1]
    for c in copies[4:]:
        c.wait()
    for side, leave in ((0, leave_zm), (1, leave_zp)):
        for b in range(ny // 8):
            rows = slice(8 * b, 8 * b + 8)
            f = [pbuf[side, i, rows] for i in range(19)]
            values = [f[i] for i in leave] + list(moments(f))
            values.append(fpbuf[side, rows].astype(jnp.float32))
            for k, v in enumerate(values):
                zsc[side, k, rows, :] = v
    up_z = 1 - lax.axis_index("wide") % 2
    up_y = 1 - lax.axis_index("narrow") % 2
    o_y1[...] = ysc[up_y]
    o_y2[...] = ysc[1 - up_y]
    o_z1[...] = zsc[up_z]
    o_z2[...] = zsc[1 - up_z]


def pack_layers(kz, ky, kx, nz, yr1, yr2, own, o_c1, o_c2, o_p, o_e, zsc):
    even = lax.axis_index("narrow") % 2 == 0
    low = pick(even, yr2[...], yr1[...])
    high = pick(even, yr1[...], yr2[...])
    lane = lax.broadcasted_iota(jnp.int32, (24, 128), 1)
    tail = jnp.zeros((24 - ky - 2 * RIM, 128), jnp.float32)
    for g in range(GROUPS):
        at = FACE * nz + RIM * g
        o_e[g, 0:RIM, :] = low[at : at + RIM]
        o_e[g, RIM : RIM + ky, :] = own[g, 0:ky, :]
        o_e[g, RIM + ky : 2 * RIM + ky, :] = high[at : at + RIM]
        o_e[g, 2 * RIM + ky : 24, :] = tail
    o_p[...] = o_e[POT]
    for side, layer, plane in ((0, 0, 0), (1, kz - 1, nz - 1)):
        zsc[side, 0:24, :] = o_e[POT]
        zsc[side, 24:48, :] = o_e[SRC]
        parts = [lanes_to(o_e[g], kx * (s - layer)) for s, g in enumerate((COND, PH, MX, MY))]
        face = pick(lane < kx, parts[0], parts[1])
        face = pick(lane < 2 * kx, face, parts[2])
        face = pick(lane < 3 * kx, face, parts[3])
        zsc[side, 48:72, :] = face
        zsc[side, 72:96, :] = o_e[MZ]
        for k in range(FACE):
            at = k * nz + plane
            zsc[side, 96 + k : 97 + k, :] = low[at : at + 1]
            zsc[side, 106 + k : 107 + k, :] = high[at : at + 1]
        zsc[side, 116:120, :] = jnp.zeros((4, 128), jnp.float32)
    up_z = 1 - lax.axis_index("wide") % 2
    o_c1[...] = zsc[up_z]
    o_c2[...] = zsc[1 - up_z]


def step_kernel(
    W,
    N,
    pops,
    flags,
    tab_hbm,
    fz1,
    fz2,
    yr1,
    yr2,
    zr1,
    zr2,
    pr_up,
    pr_dn,
    ext,
    o_pops,
    o_pot,
    o_lor,
    buf,
    fbuf,
    post,
    fc,
    fu,
    tab,
    sem_in,
    sem_out,
):
    nz, ny, nx = buf.shape[1:]
    kz, ky, kx = o_pot.shape
    wi, ni = lax.axis_index("wide"), lax.axis_index("narrow")
    tcopy = pltpu.make_async_copy(tab_hbm, tab, sem_in.at[nz + 1])
    tcopy.start()
    fcopy = pltpu.make_async_copy(flags, fbuf, sem_in.at[nz])
    fcopy.start()
    for z in range(nz):
        pltpu.make_async_copy(pops.at[:, z], buf.at[:, z], sem_in.at[z]).start()

    even_z = wi % 2 == 0
    even_y = ni % 2 == 0
    has_low_z, has_high_z = wi > 0, wi < W - 1
    has_low_y, has_high_y = ni > 0, ni < N - 1

    def z_low(rows):
        return pick(even_z, zr2[rows, :], zr1[rows, :])

    def z_high(rows):
        return pick(even_z, zr1[rows, :], zr2[rows, :])

    shape = (24, 128)
    lane = lax.broadcasted_iota(jnp.int32, shape, 1)
    row = lax.broadcasted_iota(jnp.int32, shape, 0)
    y_at = ni * ky + row - RIM
    y_in = (y_at >= 0) & (y_at < ky * N)
    layer = lane // kx
    x_at = lane - layer * kx

    def inside(first):
        z_at = wi * kz + first + layer
        return y_in & (z_at >= 0) & (z_at < kz * W) & (layer < kz)

    inner = [inside(-kz), inside(0), inside(kz)]
    beyond = [inside(-2 * kz), inside(2 * kz)]

    def group(at):
        rows = slice(24 * at, 24 * at + 24)
        return z_low(rows), z_high(rows)

    def three(g, at):
        a, b = group(at)
        return [a, ext[g], b]

    zero = jnp.zeros(shape, jnp.float32)
    field = [pick(m, v, 0.0) for m, v in zip(inner, three(POT, 0))]
    far_low = pick(beyond[0], pr_dn[...], 0.0)
    far_high = pick(beyond[1], pr_up[...], 0.0)
    source = three(SRC, 1)
    last = (kz - 1) * kx

    def next_z(here, above):
        return pick(lane < last, lanes_to(here, -kx), lanes_to(above, last))

    def prev_z(here, below):
        return pick(lane >= kx, lanes_to(here, kx), lanes_to(below, -last))

    def next_x(v):
        return pick(x_at == kx - 1, 0.0, lanes_to(v, -1))

    def prev_x(v):
        return pick(x_at == 0, 0.0, lanes_to(v, 1))

    def next_y(v):
        return pltpu.roll(v, 23, 0)

    def prev_y(v):
        return pltpu.roll(v, 1, 0)

    def sweep(values, lower, upper):
        chain = [lower] + values + [upper]
        new = []
        for k in range(3):
            v = values[k]
            total = next_z(v, chain[k + 2]) + prev_z(v, chain[k])
            total = total + next_y(v) + prev_y(v)
            total = total + next_x(v) + prev_x(v)
            new.append(pick(inner[k], (total + source[k]) / 6.0, 0.0))
        return new

    field = sweep(field, far_low, far_high)
    field = sweep(field, zero, zero)

    tcopy.wait()
    face = group(2)
    mz = three(MZ, 3)

    def face_fields(slot, g):
        k = slot
        a = lanes_to(face[0], kx * (kz - 1 - k))
        b = lanes_to(face[1], -kx * k)
        return [a, ext[g], b]

    cond = face_fields(0, COND)
    phase = face_fields(1, PH)
    mx = face_fields(2, MX)
    my = face_fields(3, MY)
    chain = [zero] + field + [zero]
    lorentz = []
    for k in range(3):
        v = field[k]
        grad = (
            (next_x(v) - prev_x(v)) * 0.5,
            (next_y(v) - prev_y(v)) * 0.5,
            (next_z(v, chain[k + 2]) - prev_z(v, chain[k])) * 0.5,
        )
        cur = []
        for a in range(3):
            applied = pick(
                phase[k] < 0.5, tab[0, 1 + a], pick(phase[k] < 1.5, tab[1, 1 + a], tab[2, 1 + a])
            )
            cur.append(cond[k] * (applied - grad[a]))
        lorentz.append(
            [
                cur[1] * mz[k] - cur[2] * my[k],
                cur[2] * mx[k] - cur[0] * mz[k],
                cur[0] * my[k] - cur[1] * mx[k],
            ]
        )
    for l in range(kz):
        o_pot[l] = lanes_to(field[1], -kx * l)[RIM : RIM + ky, 0:kx]
        for a in range(3):
            o_lor[a, l] = lanes_to(lorentz[1][a], -kx * l)[RIM : RIM + ky, 0:kx]

    src = lax.broadcasted_iota(jnp.int32, (128, 128), 0)
    dst = lax.broadcasted_iota(jnp.int32, (128, 128), 1) // (nx // kx)

    def widened(stack, l):
        choose = jnp.where(src == kx * l + dst, 1.0, 0.0)
        return lax.dot_general(
            stack,
            choose,
            (((1,), (0,)), ((), ())),
            precision=lax.Precision.HIGHEST,
            preferred_element_type=jnp.float32,
        )

    stacks = [
        jnp.concatenate([lorentz[k][a] * force_scale for a in range(3)], axis=0) for k in range(3)
    ]
    wide = [widened(stacks[0], kz - 1)]
    wide += [widened(stacks[1], l) for l in range(kz)]
    wide += [widened(stacks[2], 0)]
    sub = lax.broadcasted_iota(jnp.int32, (8, 128), 0)
    for l in range(kz + 2):
        for a in range(3):
            fc[l, a] = wide[l][24 * a : 24 * a + 24]
    for l in range(kz + 2):
        for a in range(3):
            for b in range(ny // 8):
                first = jnp.broadcast_to(fc[l, a, pl.ds(RIM + 2 * b, 1), :], (8, 128))
                second = jnp.broadcast_to(fc[l, a, pl.ds(RIM + 2 * b + 1, 1), :], (8, 128))
                fu[l, a, 8 * b : 8 * b + 8, :] = pick(sub < 4, first, second)

    def beyond_face(values, leave, force, there):
        flag = values[9]
        co = coefficients(values[5], values[6:9], force, flag < 0.5, (flag > 1.5) & (flag < 2.5))
        shut = (flag > 0.5) & (flag < 1.5)
        shut = shut | jnp.logical_not(there)
        return [(i, pick(shut, CLOSED, post_one(i, values[k], co))) for k, i in leave]

    zrow = lax.broadcasted_iota(jnp.int32, (nz, 128), 0)
    for low, leave, frow, at, there in (
        (True, leave_yp, RIM - 1, 7, has_low_y),
        (False, leave_ym, RIM + ky, 8 + ny, has_high_y),
    ):
        first, second = (yr2, yr1) if low else (yr1, yr2)
        values = [
            pick(even_y, first[nz * k : nz * k + nz, :], second[nz * k : nz * k + nz, :])
            for k in range(FACE)
        ]
        force = []
        for a in range(3):
            rows = [jnp.broadcast_to(fc[1 + l, a, frow : frow + 1, :], (nz, 128)) for l in range(kz)]
            v = rows[kz - 1]
            for l in range(kz - 2, -1, -1):
                v = pick(zrow < 4 * (l + 1), rows[l], v)
            force.append(v)
        there_b = jnp.broadcast_to(there, (nz, 128))
        for i, v in beyond_face(values, list(enumerate(leave)), force, there_b):
            for z in range(nz):
                post[i, 1 + z, at : at + 1, :] = v[z : z + 1]

    for low, leave, l, at, there in (
        (True, leave_zp, 0, 0, has_low_z),
        (False, leave_zm, kz + 1, nz + 1, has_high_z),
    ):
        first, second = (fz2, fz1) if low else (fz1, fz2)
        there_b = jnp.broadcast_to(there, (8, 128))
        for b in range(ny // 8):
            rows = slice(8 * b, 8 * b + 8)
            values = [pick(even_z, first[k, rows, :], second[k, rows, :]) for k in range(FACE)]
            force = [fu[l, a, rows, :] for a in range(3)]
            for i, v in beyond_face(values, list(enumerate(leave)), force, there_b):
                post[i, at, 8 + 8 * b : 16 + 8 * b, :] = v

    for z_side, y_side, i, k, there in (
        (0, 0, 15, 3, has_low_z & has_low_y),
        (0, 1, 18, 4, has_low_z & has_high_y),
        (1, 0, 17, 4, has_high_z & has_low_y),
        (1, 1, 16, 3, has_high_z & has_high_y),
    ):
        at = 96 + FACE * y_side
        rows = (z_high if z_side else z_low)(slice(at, at + FACE))
        values = [rows[j : j + 1] for j in range(FACE)]
        frow = RIM + ky if y_side else RIM - 1
        force = [fc[(kz + 1) * z_side, a, frow : frow + 1, :] for a in range(3)]
        there_b = jnp.broadcast_to(there, (1, 128))
        for i, v in beyond_face(values, [(k, i)], force, there_b):
            yrow = 8 + ny if y_side else 7
            post[i, (nz + 1) * z_side, yrow : yrow + 1, :] = v

    fcopy.wait()

    def collide(z, carry):
        pltpu.make_async_copy(pops.at[:, z], buf.at[:, z], sem_in.at[z]).wait()
        l = 1 + z // 4
        for b in range(ny // 8):
            rows = slice(8 * b, 8 * b + 8)
            out = slice(8 + 8 * b, 16 + 8 * b)
            f = [buf[i, z, rows, :] for i in range(19)]
            flag = fbuf[z, rows, :]
            force = [fu[l, a, rows, :] for a in range(3)]
            rho, mom_x, mom_y, mom_z = moments(f)
            wall = flag == 1
            co = coefficients(rho, (mom_x, mom_y, mom_z), force, flag == 0, flag == 2)
            keep = co[0]
            post[0, 1 + z, out, :] = pick(wall, CLOSED, keep * f[0] + 12.0 * co[1])
            for i, j in pairs:
                sym, anti = post_pair(i, co)
                post[i, 1 + z, out, :] = pick(wall, CLOSED, keep * f[i] + (sym + anti))
                post[j, 1 + z, out, :] = pick(wall, CLOSED, keep * f[j] + (sym - anti))
        return carry

    lax.fori_loop(0, nz, collide, 0)

    lane8 = lax.broadcasted_iota(jnp.int32, (8, 128), 1)
    not_first = lane8 > 0
    not_last = lane8 < nx - 1

    def passing(z, carry):
        for b in range(ny // 8):
            rows = slice(8 * b, 8 * b + 8)
            out = slice(8 + 8 * b, 16 + 8 * b)
            wall = fbuf[z, rows, :] == 1
            for i in range(19):
                cx, cy, cz = lattice_dirs[i]
                own = post[opposite_dir[i], 1 + z, out, :]
                if i > 0:
                    v = post[i, 1 + z - cz, 8 + 8 * b - cy : 16 + 8 * b - cy, :]
                    if cx != 0:
                        v = pltpu.roll(v, cx % nx, 1)
                    ok = v > OPEN_ABOVE
                    if cx == 1:
                        ok = ok & not_first
                    if cx == -1:
                        ok = ok & not_last
                    own = pick(ok, v, own)
                buf[i, z, rows, :] = pick(wall, buf[i, z, rows, :], own)
        pltpu.make_async_copy(buf.at[:, z], o_pops.at[:, z], sem_out.at[z]).start()
        return carry

    lax.fori_loop(0, nz, passing, 0)

    def drain(z, carry):
        pltpu.make_async_copy(buf.at[:, z], o_pops.at[:, z], sem_out.at[z]).wait()
        return carry

    lax.fori_loop(0, nz, drain, 0)


def pair_first(size):
    return [(i, i ^ 1) for i in range(size)]


def pair_second(size, wrap):
    found = []
    for i in range(1, size, 2):
        j = (i + 1) % size
        if j > i or wrap:
            found += [(i, j), (j, i)]
    return found


def solution(mesh):
    W, N = mesh.shape["wide"], mesh.shape["narrow"]

    def per_device(populations, flags, potential, conductivity, coil_phase, phase_table, magnetic):
        f32 = jnp.float32
        nz, ny, nx = flags.shape
        kz, ky, kx = potential.shape
        yrows = FACE * nz + RIM * GROUPS
        yrows += -yrows % 8
        params = pltpu.CompilerParams(vmem_limit_bytes=VMEM_LIMIT)
        shape = jax.ShapeDtypeStruct
        z1, z2, y1, y2, own = pl.pallas_call(
            pack_faces,
            name="pack_faces",
            out_shape=(
                shape((FACE, ny, nx), f32),
                shape((FACE, ny, nx), f32),
                shape((yrows, nx), f32),
                shape((yrows, nx), f32),
                shape((GROUPS, 16, nx), f32),
            ),
            in_specs=[hbm_spec] * 7,
            out_specs=[vmem_spec] * 5,
            scratch_shapes=[
                pltpu.VMEM((2, 19, ny, nx), f32),
                pltpu.VMEM((2, 19, nz, 8, nx), f32),
                pltpu.VMEM((2, ny, nx), jnp.int32),
                pltpu.VMEM((2, nz, 8, nx), jnp.int32),
                pltpu.VMEM((2, FACE, ny, nx), f32),
                pltpu.VMEM((2, yrows, nx), f32),
                pltpu.VMEM(potential.shape, f32),
                pltpu.VMEM(conductivity.shape, f32),
                pltpu.VMEM(coil_phase.shape, jnp.int32),
                pltpu.VMEM(magnetic.shape, f32),
                pltpu.SMEM(phase_table.shape, f32),
                pltpu.SemaphoreType.DMA((13,)),
            ],
            compiler_params=params,
        )(
            *[
                pltpu.with_memory_space_constraint(x, pltpu.HBM)
                for x in (populations, flags, potential, conductivity, coil_phase, magnetic, phase_table)
            ]
        )
        yr1 = lax.ppermute(y1, "narrow", pair_first(N))
        yr2 = lax.ppermute(y2, "narrow", pair_second(N, True))
        fz1 = lax.ppermute(z1, "wide", pair_first(W))
        fz2 = lax.ppermute(z2, "wide", pair_second(W, False))
        c1, c2, pot_rows, ext = pl.pallas_call(
            lambda *refs: pack_layers(kz, ky, kx, nz, *refs),
            name="pack_layers",
            out_shape=(
                shape((120, nx), f32),
                shape((120, nx), f32),
                shape((24, nx), f32),
                shape((GROUPS, 24, nx), f32),
            ),
            in_specs=[vmem_spec] * 3,
            out_specs=[vmem_spec] * 4,
            scratch_shapes=[pltpu.VMEM((2, 120, nx), f32)],
            compiler_params=params,
        )(yr1, yr2, own)
        zr1 = lax.ppermute(c1, "wide", pair_first(W))
        zr2 = lax.ppermute(c2, "wide", pair_second(W, False))
        if W == 4:
            pr_up = lax.ppermute(pot_rows, "wide", [(i, i ^ 2) for i in range(W)])
            pr_dn = pr_up
        else:
            pr_up = lax.ppermute(pot_rows, "wide", [(i, i - 2) for i in range(2, W)])
            pr_dn = lax.ppermute(pot_rows, "wide", [(i, i + 2) for i in range(W - 2)])
        return pl.pallas_call(
            lambda *refs: step_kernel(W, N, *refs),
            name="mold_step",
            out_shape=(
                shape(populations.shape, f32),
                shape(potential.shape, f32),
                shape(magnetic.shape, f32),
            ),
            in_specs=[any_spec] * 3 + [vmem_spec] * 9,
            out_specs=[any_spec, vmem_spec, vmem_spec],
            scratch_shapes=[
                pltpu.VMEM(populations.shape, f32),
                pltpu.VMEM(flags.shape, jnp.int32),
                pltpu.VMEM((19, nz + 2, ny + 16, nx), f32),
                pltpu.VMEM((kz + 2, 3, 24, nx), f32),
                pltpu.VMEM((kz + 2, 3, ny, nx), f32),
                pltpu.SMEM(phase_table.shape, f32),
                pltpu.SemaphoreType.DMA((nz + 2,)),
                pltpu.SemaphoreType.DMA((nz,)),
            ],
            compiler_params=params,
        )(
            populations,
            flags,
            phase_table,
            fz1,
            fz2,
            yr1,
            yr2,
            zr1,
            zr2,
            pr_up,
            pr_dn,
            ext,
        )

    in_specs = (
        P(None, ("groups", "wide"), "narrow", None),
        P(("groups", "wide"), "narrow", None),
        P(("groups", "wide"), "narrow", None),
        P(("groups", "wide"), "narrow", None),
        P(("groups", "wide"), "narrow", None),
        P(),
        P(None, ("groups", "wide"), "narrow", None),
    )
    out_specs = (
        P(None, ("groups", "wide"), "narrow", None),
        P(("groups", "wide"), "narrow", None),
        P(None, ("groups", "wide"), "narrow", None),
    )
    return jax.shard_map(
        per_device, mesh=mesh, in_specs=in_specs, out_specs=out_specs, check_vma=False
    )
```

```python
import jax
import jax.numpy as jnp
from jax import lax
from jax.experimental import pallas as pl
from jax.experimental.pallas import tpu as pltpu
from jax.sharding import PartitionSpec as P

lattice_dirs = [
    (0, 0, 0),
    (1, 0, 0),
    (-1, 0, 0),
    (0, 1, 0),
    (0, -1, 0),
    (0, 0, 1),
    (0, 0, -1),
    (1, 1, 0),
    (-1, -1, 0),
    (1, -1, 0),
    (-1, 1, 0),
    (1, 0, 1),
    (-1, 0, -1),
    (1, 0, -1),
    (-1, 0, 1),
    (0, 1, 1),
    (0, -1, -1),
    (0, 1, -1),
    (0, -1, 1),
]
opposite_dir = [0, 2, 1, 4, 3, 6, 5, 8, 7, 10, 9, 12, 11, 14, 13, 16, 15, 18, 17]
pairs = [(i, opposite_dir[i]) for i in range(1, 19) if i < opposite_dir[i]]
relax_time = 0.8
force_scale = 0.02
inlet_speed = 0.05
force_factor = 1.0 - 0.5 / relax_time

leave_yp = [3, 7, 10, 15, 17]
leave_ym = [4, 8, 9, 16, 18]
leave_zp = [5, 11, 14, 15, 18]
leave_zm = [6, 12, 13, 16, 17]

FACE = 10
GROUPS = 7
POT, SRC, COND, PH, MX, MY, MZ = range(GROUPS)
RIM = 4
CLOSED = -1e30
OPEN_ABOVE = -1e29
WRAP_COARSE = True
VMEM_LIMIT = 32 * 1024 * 1024

any_spec = pl.BlockSpec(memory_space=pl.ANY)
hbm_spec = pl.BlockSpec(memory_space=pltpu.HBM)
vmem_spec = pl.BlockSpec(memory_space=pltpu.VMEM)


def moments(f):
    d = {}
    rho = f[0]
    for i, j in pairs:
        rho = rho + (f[i] + f[j])
        d[i] = f[i] - f[j]
    mx = d[1] + d[7] + d[9] + d[11] + d[13]
    my = d[3] + d[7] - d[9] + d[15] + d[17]
    mz = d[5] + d[11] - d[13] + d[15] - d[17]
    return rho, mx, my, mz


def coefficients(rho, mom, force, fluid, inlet):
    inv = 1.0 / rho
    u = [(m + 0.5 * f) * inv for m, f in zip(mom, force)]
    u = [jnp.where(inlet, c, v) for c, v in zip((0.0, 0.0, -inlet_speed), u)]
    r = jnp.where(fluid, rho * (1.0 / (36.0 * relax_time)), 1.0 / 36.0)
    f = [jnp.where(fluid, v * (force_factor / 36.0), 0.0) for v in force]
    sq = u[0] * u[0] + u[1] * u[1] + u[2] * u[2]
    uf = u[0] * f[0] + u[1] * f[1] + u[2] * f[2]
    base = r * (1.0 - 1.5 * sq) - 3.0 * uf
    ru = [r * v for v in u]
    g = [4.5 * a + 9.0 * b for a, b in zip(ru, f)]
    h = [3.0 * (a + b) for a, b in zip(ru, f)]
    keep = jnp.where(fluid, 1.0 - 1.0 / relax_time, 0.0)
    return keep, base, u, g, h


def along(c, v):
    total = None
    for s, x in zip(c, v):
        if s == 0:
            continue
        if total is None:
            total = x if s > 0 else -x
        else:
            total = total + x if s > 0 else total - x
    return total


def post_pair(i, co):
    keep, base, u, g, h = co
    c = lattice_dirs[i]
    sym = base + along(c, u) * along(c, g)
    anti = along(c, h)
    if sum(abs(s) for s in c) == 1:
        return 2.0 * sym, 2.0 * anti
    return sym, anti


def post_one(i, f, co):
    keep = co[0]
    if i < opposite_dir[i]:
        sym, anti = post_pair(i, co)
        return keep * f + (sym + anti)
    sym, anti = post_pair(opposite_dir[i], co)
    return keep * f + (sym - anti)


def pick(cond, a, b):
    return jnp.where(cond, a, b)


def lanes_to(x, shift):
    shift = shift % 128
    return x if shift == 0 else pltpu.roll(x, shift, 1)


def z_sections(ky):
    return [ky * g for g in range(4)] + [4 * ky]


def y_sections(nz):
    found, at = [], FACE * nz
    own = [RIM, RIM, 1, 1, 1, 1, 1]
    side = [RIM, RIM, 1, 1]
    for rows in own + side + side + [1, 1, FACE, FACE]:
        found.append((at, rows))
        at += rows
    return found, at + -at % 8


def pack_coarse(
    pops,
    flags,
    pot_hbm,
    cond_hbm,
    ph_hbm,
    mag_hbm,
    tab_hbm,
    o_c1,
    o_c2,
    o_g,
    o_p,
    ebuf,
    febuf,
    zsc,
    pot,
    cond,
    ph,
    mag,
    tab,
    sems,
):
    nz, ny = pops.shape[1], pops.shape[2]
    kz, ky, kx = pot.shape
    coarse = [
        pltpu.make_async_copy(a, b, sems.at[8 + k])
        for k, (a, b) in enumerate(
            ((tab_hbm, tab), (ph_hbm, ph), (cond_hbm, cond), (pot_hbm, pot), (mag_hbm, mag))
        )
    ]
    copies = []
    for k, (plane, row) in enumerate(((0, 0), (0, ny - 8), (nz - 1, 0), (nz - 1, ny - 8))):
        rows = pl.ds(row, 8)
        copies.append(pltpu.make_async_copy(pops.at[:, plane, rows, :], ebuf.at[k], sems.at[k]))
        copies.append(pltpu.make_async_copy(flags.at[plane, rows, :], febuf.at[k], sems.at[4 + k]))
    for c in coarse + copies:
        c.start()
    for c in coarse:
        c.wait()
    phase = ph[...]
    conductivity = cond[...]
    source = conductivity * jnp.where(
        phase == 0, tab[0, 0], jnp.where(phase == 1, tab[1, 0], tab[2, 0])
    )
    fields = [pot[...], source, conductivity, phase.astype(jnp.float32), mag[0], mag[1], mag[2]]
    blank = jnp.zeros((ky, 128 - kz * kx), jnp.float32)
    rows = []
    for g, field in enumerate(fields):
        rows.append(jnp.concatenate([field[l] for l in range(kz)] + [blank], axis=1))
        o_g[g, 0:ky, :] = rows[g]
    o_p[0:ky, :] = rows[POT]
    o_p[ky:16, :] = jnp.zeros((16 - ky, 128), jnp.float32)
    at = z_sections(ky)
    for side, layer in ((0, 0), (1, kz - 1)):
        face = [fields[g][layer] for g in (COND, PH, MX, MY)]
        face = jnp.concatenate(face, axis=1)
        for k, v in enumerate((rows[POT], rows[SRC], face, rows[MZ])):
            zsc[side, at[k] : at[k] + ky, :] = v
    for c in copies:
        c.wait()
    for side, leave in ((0, leave_zm), (1, leave_zp)):
        for y_side, row in ((0, 0), (1, 7)):
            f = [ebuf[2 * side + y_side, i] for i in range(19)]
            values = [f[i] for i in leave] + list(moments(f))
            values.append(febuf[2 * side + y_side].astype(jnp.float32))
            for k, v in enumerate(values):
                to = at[4] + FACE * y_side + k
                zsc[side, to : to + 1, :] = v[row : row + 1]
        zsc[side, at[4] + 2 * FACE :, :] = jnp.zeros(
            (zsc.shape[1] - at[4] - 2 * FACE, 128), jnp.float32
        )
    up_z = 1 - lax.axis_index("wide") % 2
    o_c1[...] = zsc[up_z]
    o_c2[...] = zsc[1 - up_z]


def pack_faces(pops, flags, after, o_z1, o_z2, o_y, pbuf, ybuf, fpbuf, fybuf, zsc, sems):
    nz, ny = pops.shape[1], pops.shape[2]
    copies = []
    for side, plane in ((0, 0), (1, nz - 1)):
        copies.append(pltpu.make_async_copy(pops.at[:, plane], pbuf.at[side], sems.at[side]))
        copies.append(pltpu.make_async_copy(flags.at[plane], fpbuf.at[side], sems.at[2 + side]))
    for side, row in ((0, 0), (1, ny - 8)):
        rows = pl.ds(row, 8)
        copies.append(pltpu.make_async_copy(pops.at[:, :, rows, :], ybuf.at[side], sems.at[4 + side]))
        copies.append(pltpu.make_async_copy(flags.at[:, rows, :], fybuf.at[side], sems.at[6 + side]))
    for c in copies:
        c.start()
    for c in copies[:4]:
        c.wait()
    for side, leave in ((0, leave_zm), (1, leave_zp)):
        for b in range(ny // 8):
            rows = slice(8 * b, 8 * b + 8)
            f = [pbuf[side, i, rows] for i in range(19)]
            values = [f[i] for i in leave] + list(moments(f))
            values.append(fpbuf[side, rows].astype(jnp.float32))
            for k, v in enumerate(values):
                zsc[side, k, rows, :] = v
    up_z = 1 - lax.axis_index("wide") % 2
    o_z1[...] = zsc[up_z]
    o_z2[...] = zsc[1 - up_z]
    for c in copies[4:]:
        c.wait()
    for side, leave, row in ((0, leave_ym, 0), (1, leave_yp, 7)):
        for z in range(nz):
            f = [ybuf[side, i, z] for i in range(19)]
            values = [f[i] for i in leave] + list(moments(f))
            values.append(fybuf[side, z].astype(jnp.float32))
            for k, v in enumerate(values):
                o_y[side, k * nz + z : k * nz + z + 1, :] = v[row : row + 1]


def pack_rows(kz, ky, nz, zr1, zr2, pr_up, pr_dn, own, fine, o_y1, o_y2, ysc):
    even = lax.axis_index("wide") % 2 == 0
    low = pick(even, zr2[...], zr1[...])
    high = pick(even, zr1[...], zr2[...])
    zat = z_sections(ky)
    sections, total = y_sections(nz)
    blocks = [own[g, 0:ky, :] for g in range(GROUPS)]
    blocks += [low[a : a + ky] for a in zat[:4]]
    blocks += [high[a : a + ky] for a in zat[:4]]
    blocks += [pr_dn[0:ky, :], pr_up[0:ky, :]]
    for side in range(2):
        ysc[side, 0 : FACE * nz, :] = fine[side]
        for (at, rows), v in zip(sections, blocks):
            ysc[side, at : at + rows, :] = v[ky - rows : ky] if side else v[0:rows]
        for (at, rows), v in zip(sections[len(blocks) :], (low, high)):
            first = zat[4] + FACE * side
            ysc[side, at : at + rows, :] = v[first : first + FACE]
        used = sections[-1][0] + FACE
        if used < total:
            ysc[side, used:total, :] = jnp.zeros((total - used, 128), jnp.float32)
    up_y = 1 - lax.axis_index("narrow") % 2
    o_y1[...] = ysc[up_y]
    o_y2[...] = ysc[1 - up_y]


def step_kernel(
    W,
    N,
    pops,
    flags,
    tab_hbm,
    fz1,
    fz2,
    yr1,
    yr2,
    zr1,
    zr2,
    pr_up,
    pr_dn,
    own,
    o_pops,
    o_pot,
    o_lor,
    obuf,
    ext,
    post,
    fc,
    fu,
    tab,
    sem_tab,
    sem_out,
):
    nz, ny, nx = obuf.shape[1:]
    kz, ky, kx = o_pot.shape
    wi, ni = lax.axis_index("wide"), lax.axis_index("narrow")
    tcopy = pltpu.make_async_copy(tab_hbm, tab, sem_tab)
    tcopy.start()
    even_z = wi % 2 == 0
    even_y = ni % 2 == 0
    has_low_z, has_high_z = wi > 0, wi < W - 1
    has_low_y, has_high_y = ni > 0, ni < N - 1

    z_lo = pick(even_z, zr2[...], zr1[...])
    z_hi = pick(even_z, zr1[...], zr2[...])
    y_lo = pick(even_y, yr2[...], yr1[...])
    y_hi = pick(even_y, yr1[...], yr2[...])
    zat = z_sections(ky)
    sections, _ = y_sections(nz)
    blocks = [own[g, 0:ky, :] for g in range(GROUPS)]
    blocks += [z_lo[a : a + ky] for a in zat[:4]]
    blocks += [z_hi[a : a + ky] for a in zat[:4]]
    blocks += [pr_dn[0:ky, :], pr_up[0:ky, :]]
    blank = jnp.zeros((RIM, 128), jnp.float32)
    for k, ((at, rows), v) in enumerate(zip(sections, blocks)):
        if rows < RIM:
            ext[k, 0:RIM, :] = blank
            ext[k, RIM + ky : 2 * RIM + ky, :] = blank
        ext[k, RIM - rows : RIM, :] = y_lo[at : at + rows]
        ext[k, RIM : RIM + ky, :] = v
        ext[k, RIM + ky : RIM + ky + rows, :] = y_hi[at : at + rows]
        ext[k, 2 * RIM + ky : 24, :] = jnp.zeros((24 - 2 * RIM - ky, 128), jnp.float32)
    below, above, far = GROUPS, GROUPS + 4, GROUPS + 8

    shape = (24, 128)
    lane = lax.broadcasted_iota(jnp.int32, shape, 1)
    row = lax.broadcasted_iota(jnp.int32, shape, 0)
    y_at = ni * ky + row - RIM
    y_in = (y_at >= 0) & (y_at < ky * N)
    layer = lane // kx
    x_at = lane - layer * kx

    def inside(first):
        z_at = wi * kz + first + layer
        return y_in & (z_at >= 0) & (z_at < kz * W) & (layer < kz)

    inner = [inside(-kz), inside(0), inside(kz)]
    beyond = [inside(-2 * kz), inside(2 * kz)]

    def three(g, at):
        return [ext[below + at], ext[g], ext[above + at]]

    zero = jnp.zeros(shape, jnp.float32)
    field = [pick(m, v, 0.0) for m, v in zip(inner, three(POT, 0))]
    far_low = pick(beyond[0], ext[far], 0.0)
    far_high = pick(beyond[1], ext[far + 1], 0.0)
    source = three(SRC, 1)
    last = (kz - 1) * kx

    def next_z(here, above):
        return pick(lane < last, lanes_to(here, -kx), lanes_to(above, last))

    def prev_z(here, below):
        return pick(lane >= kx, lanes_to(here, kx), lanes_to(below, -last))

    def next_x(v):
        return pick(x_at == kx - 1, 0.0, lanes_to(v, -1))

    def prev_x(v):
        return pick(x_at == 0, 0.0, lanes_to(v, 1))

    def next_y(v):
        return pltpu.roll(v, 23, 0)

    def prev_y(v):
        return pltpu.roll(v, 1, 0)

    def sweep(values, lower, upper):
        chain = [lower] + values + [upper]
        new = []
        for k in range(3):
            v = values[k]
            total = next_z(v, chain[k + 2]) + prev_z(v, chain[k])
            total = total + next_y(v) + prev_y(v)
            total = total + next_x(v) + prev_x(v)
            new.append(pick(inner[k], (total + source[k]) / 6.0, 0.0))
        return new

    field = sweep(field, far_low, far_high)
    field = sweep(field, zero, zero)

    tcopy.wait()
    face = ext[below + 2], ext[above + 2]
    mz = three(MZ, 3)

    def face_fields(slot, g):
        k = slot
        a = lanes_to(face[0], kx * (kz - 1 - k))
        b = lanes_to(face[1], -kx * k)
        return [a, ext[g], b]

    cond = face_fields(0, COND)
    phase = face_fields(1, PH)
    mx = face_fields(2, MX)
    my = face_fields(3, MY)
    chain = [zero] + field + [zero]
    lorentz = []
    for k in range(3):
        v = field[k]
        grad = (
            (next_x(v) - prev_x(v)) * 0.5,
            (next_y(v) - prev_y(v)) * 0.5,
            (next_z(v, chain[k + 2]) - prev_z(v, chain[k])) * 0.5,
        )
        cur = []
        for a in range(3):
            applied = pick(
                phase[k] < 0.5, tab[0, 1 + a], pick(phase[k] < 1.5, tab[1, 1 + a], tab[2, 1 + a])
            )
            cur.append(cond[k] * (applied - grad[a]))
        lorentz.append(
            [
                cur[1] * mz[k] - cur[2] * my[k],
                cur[2] * mx[k] - cur[0] * mz[k],
                cur[0] * my[k] - cur[1] * mx[k],
            ]
        )
    for l in range(kz):
        o_pot[l] = lanes_to(field[1], -kx * l)[RIM : RIM + ky, 0:kx]
        for a in range(3):
            o_lor[a, l] = lanes_to(lorentz[1][a], -kx * l)[RIM : RIM + ky, 0:kx]

    src = lax.broadcasted_iota(jnp.int32, (128, 128), 0)
    dst = lax.broadcasted_iota(jnp.int32, (128, 128), 1) // (nx // kx)

    def widened(stack, l):
        choose = jnp.where(src == kx * l + dst, 1.0, 0.0)
        return lax.dot_general(
            stack,
            choose,
            (((1,), (0,)), ((), ())),
            precision=lax.Precision.HIGHEST,
            preferred_element_type=jnp.float32,
        )

    stacks = [
        jnp.concatenate([lorentz[k][a] * force_scale for a in range(3)], axis=0) for k in range(3)
    ]
    wide = [widened(stacks[0], kz - 1)]
    wide += [widened(stacks[1], l) for l in range(kz)]
    wide += [widened(stacks[2], 0)]
    sub = lax.broadcasted_iota(jnp.int32, (8, 128), 0)
    for l in range(kz + 2):
        for a in range(3):
            fc[l, a] = wide[l][24 * a : 24 * a + 24]
    for l in range(kz + 2):
        for a in range(3):
            for b in range(ny // 8):
                first = jnp.broadcast_to(fc[l, a, pl.ds(RIM + 2 * b, 1), :], (8, 128))
                second = jnp.broadcast_to(fc[l, a, pl.ds(RIM + 2 * b + 1, 1), :], (8, 128))
                fu[l, a, 8 * b : 8 * b + 8, :] = pick(sub < 4, first, second)

    def beyond_face(values, leave, force, there):
        flag = values[9]
        co = coefficients(values[5], values[6:9], force, flag < 0.5, (flag > 1.5) & (flag < 2.5))
        shut = (flag > 0.5) & (flag < 1.5)
        shut = shut | jnp.logical_not(there)
        return [(i, pick(shut, CLOSED, post_one(i, values[k], co))) for k, i in leave]

    zrow = lax.broadcasted_iota(jnp.int32, (nz, 128), 0)
    for low, leave, frow, at, there in (
        (True, leave_yp, RIM - 1, 7, has_low_y),
        (False, leave_ym, RIM + ky, 8 + ny, has_high_y),
    ):
        side = y_lo if low else y_hi
        values = [side[nz * k : nz * k + nz] for k in range(FACE)]
        force = []
        for a in range(3):
            rows = [jnp.broadcast_to(fc[1 + l, a, frow : frow + 1, :], (nz, 128)) for l in range(kz)]
            v = rows[kz - 1]
            for l in range(kz - 2, -1, -1):
                v = pick(zrow < 4 * (l + 1), rows[l], v)
            force.append(v)
        there_b = jnp.broadcast_to(there, (nz, 128))
        for i, v in beyond_face(values, list(enumerate(leave)), force, there_b):
            for z in range(nz):
                post[i, 1 + z, at : at + 1, :] = v[z : z + 1]

    for low, leave, l, at, there in (
        (True, leave_zp, 0, 0, has_low_z),
        (False, leave_zm, kz + 1, nz + 1, has_high_z),
    ):
        first, second = (fz2, fz1) if low else (fz1, fz2)
        there_b = jnp.broadcast_to(there, (8, 128))
        for b in range(ny // 8):
            rows = slice(8 * b, 8 * b + 8)
            values = [pick(even_z, first[k, rows, :], second[k, rows, :]) for k in range(FACE)]
            force = [fu[l, a, rows, :] for a in range(3)]
            for i, v in beyond_face(values, list(enumerate(leave)), force, there_b):
                post[i, at, 8 + 8 * b : 16 + 8 * b, :] = v

    for z_side, y_side, i, k, there in (
        (0, 0, 15, 3, has_low_z & has_low_y),
        (0, 1, 18, 4, has_low_z & has_high_y),
        (1, 0, 17, 4, has_high_z & has_low_y),
        (1, 1, 16, 3, has_high_z & has_high_y),
    ):
        at = sections[GROUPS + 10 + z_side][0]
        rows = (y_hi if y_side else y_lo)[at : at + FACE]
        values = [rows[j : j + 1] for j in range(FACE)]
        frow = RIM + ky if y_side else RIM - 1
        force = [fc[(kz + 1) * z_side, a, frow : frow + 1, :] for a in range(3)]
        there_b = jnp.broadcast_to(there, (1, 128))
        for i, v in beyond_face(values, [(k, i)], force, there_b):
            yrow = 8 + ny if y_side else 7
            post[i, (nz + 1) * z_side, yrow : yrow + 1, :] = v

    lane8 = lax.broadcasted_iota(jnp.int32, (8, 128), 1)
    not_first = lane8 > 0
    not_last = lane8 < nx - 1

    def collide(z):
        l = 1 + z // 4
        for b in range(ny // 8):
            rows = slice(8 * b, 8 * b + 8)
            out = slice(8 + 8 * b, 16 + 8 * b)
            f = [pops[i, z, rows, :] for i in range(19)]
            flag = flags[z, rows, :]
            force = [fu[l, a, rows, :] for a in range(3)]
            rho, mom_x, mom_y, mom_z = moments(f)
            wall = flag == 1
            co = coefficients(rho, (mom_x, mom_y, mom_z), force, flag == 0, flag == 2)
            keep = co[0]
            post[0, 1 + z, out, :] = pick(wall, CLOSED, keep * f[0] + 12.0 * co[1])
            for i, j in pairs:
                sym, anti = post_pair(i, co)
                post[i, 1 + z, out, :] = pick(wall, CLOSED, keep * f[i] + (sym + anti))
                post[j, 1 + z, out, :] = pick(wall, CLOSED, keep * f[j] + (sym - anti))

    def passing(z):
        for b in range(ny // 8):
            rows = slice(8 * b, 8 * b + 8)
            out = slice(8 + 8 * b, 16 + 8 * b)
            wall = flags[z, rows, :] == 1
            for i in range(19):
                cx, cy, cz = lattice_dirs[i]
                own = post[opposite_dir[i], 1 + z, out, :]
                if i > 0:
                    v = post[i, 1 + z - cz, 8 + 8 * b - cy : 16 + 8 * b - cy, :]
                    if cx != 0:
                        v = pltpu.roll(v, cx % nx, 1)
                    ok = v > OPEN_ABOVE
                    if cx == 1:
                        ok = ok & not_first
                    if cx == -1:
                        ok = ok & not_last
                    own = pick(ok, v, own)
                obuf[i, z, rows, :] = pick(wall, pops[i, z, rows, :], own)
        pltpu.make_async_copy(obuf.at[:, z], o_pops.at[:, z], sem_out.at[z]).start()

    collide(0)

    def plane(z, carry):
        collide(z + 1)
        passing(z)
        return carry

    lax.fori_loop(0, nz - 1, plane, 0)
    passing(nz - 1)

    def drain(z, carry):
        pltpu.make_async_copy(obuf.at[:, z], o_pops.at[:, z], sem_out.at[z]).wait()
        return carry

    lax.fori_loop(0, nz, drain, 0)


def pair_first(size):
    return [(i, i ^ 1) for i in range(size)]


def pair_second(size, wrap):
    found = []
    for i in range(1, size, 2):
        j = (i + 1) % size
        if j > i or wrap:
            found += [(i, j), (j, i)]
    return found


def solution(mesh):
    W, N = mesh.shape["wide"], mesh.shape["narrow"]

    def per_device(populations, flags, potential, conductivity, coil_phase, phase_table, magnetic):
        f32 = jnp.float32
        nz, ny, nx = flags.shape
        kz, ky, kx = potential.shape
        zrows = z_sections(ky)[4] + 2 * FACE
        zrows += -zrows % 8
        yrows = y_sections(nz)[1]
        params = pltpu.CompilerParams(vmem_limit_bytes=VMEM_LIMIT)
        shape = jax.ShapeDtypeStruct

        def in_hbm(*xs):
            return [pltpu.with_memory_space_constraint(x, pltpu.HBM) for x in xs]

        c1, c2, own, pot_rows = pl.pallas_call(
            pack_coarse,
            name="pack_coarse",
            out_shape=(
                shape((zrows, nx), f32),
                shape((zrows, nx), f32),
                shape((GROUPS, 16, nx), f32),
                shape((16, nx), f32),
            ),
            in_specs=[hbm_spec] * 7,
            out_specs=[vmem_spec] * 4,
            scratch_shapes=[
                pltpu.VMEM((4, 19, 8, nx), f32),
                pltpu.VMEM((4, 8, nx), jnp.int32),
                pltpu.VMEM((2, zrows, nx), f32),
                pltpu.VMEM(potential.shape, f32),
                pltpu.VMEM(conductivity.shape, f32),
                pltpu.VMEM(coil_phase.shape, jnp.int32),
                pltpu.VMEM(magnetic.shape, f32),
                pltpu.SMEM(phase_table.shape, f32),
                pltpu.SemaphoreType.DMA((13,)),
            ],
            compiler_params=params,
        )(
            *in_hbm(populations, flags, potential, conductivity, coil_phase, magnetic, phase_table)
        )
        zr1 = lax.ppermute(c1, "wide", pair_first(W))
        zr2 = lax.ppermute(c2, "wide", pair_second(W, WRAP_COARSE))
        if W == 4:
            pr_up = lax.ppermute(pot_rows, "wide", [(i, i ^ 2) for i in range(W)])
            pr_dn = pr_up
        else:
            pr_up = lax.ppermute(pot_rows, "wide", [(i, i - 2) for i in range(2, W)])
            pr_dn = lax.ppermute(pot_rows, "wide", [(i, i + 2) for i in range(W - 2)])
        z1, z2, fine = pl.pallas_call(
            pack_faces,
            name="pack_faces",
            out_shape=(
                shape((FACE, ny, nx), f32),
                shape((FACE, ny, nx), f32),
                shape((2, FACE * nz, nx), f32),
            ),
            in_specs=[hbm_spec] * 2 + [any_spec],
            out_specs=[vmem_spec] * 3,
            scratch_shapes=[
                pltpu.VMEM((2, 19, ny, nx), f32),
                pltpu.VMEM((2, 19, nz, 8, nx), f32),
                pltpu.VMEM((2, ny, nx), jnp.int32),
                pltpu.VMEM((2, nz, 8, nx), jnp.int32),
                pltpu.VMEM((2, FACE, ny, nx), f32),
                pltpu.SemaphoreType.DMA((8,)),
            ],
            compiler_params=params,
        )(*in_hbm(populations, flags), own)
        z1, z2, fine, zr1, zr2, pr_up, pr_dn = lax.optimization_barrier(
            (z1, z2, fine, zr1, zr2, pr_up, pr_dn)
        )
        fz1 = lax.ppermute(z1, "wide", pair_first(W))
        fz2 = lax.ppermute(z2, "wide", pair_second(W, False))
        y1, y2 = pl.pallas_call(
            lambda *refs: pack_rows(kz, ky, nz, *refs),
            name="pack_rows",
            out_shape=(shape((yrows, nx), f32), shape((yrows, nx), f32)),
            in_specs=[vmem_spec] * 6,
            out_specs=[vmem_spec] * 2,
            scratch_shapes=[pltpu.VMEM((2, yrows, nx), f32)],
            compiler_params=params,
        )(zr1, zr2, pr_up, pr_dn, own, fine)
        yr1 = lax.ppermute(y1, "narrow", pair_first(N))
        yr2 = lax.ppermute(y2, "narrow", pair_second(N, True))
        return pl.pallas_call(
            lambda *refs: step_kernel(W, N, *refs),
            name="mold_step",
            out_shape=(
                shape(populations.shape, f32),
                shape(potential.shape, f32),
                shape(magnetic.shape, f32),
            ),
            in_specs=[vmem_spec] * 2 + [any_spec] + [vmem_spec] * 9,
            out_specs=[any_spec, vmem_spec, vmem_spec],
            scratch_shapes=[
                pltpu.VMEM(populations.shape, f32),
                pltpu.VMEM((GROUPS + 10, 24, nx), f32),
                pltpu.VMEM((19, nz + 2, ny + 16, nx), f32),
                pltpu.VMEM((kz + 2, 3, 24, nx), f32),
                pltpu.VMEM((kz + 2, 3, ny, nx), f32),
                pltpu.SMEM(phase_table.shape, f32),
                pltpu.SemaphoreType.DMA,
                pltpu.SemaphoreType.DMA((nz,)),
            ],
            compiler_params=params,
        )(
            pltpu.with_memory_space_constraint(populations, pltpu.VMEM),
            pltpu.with_memory_space_constraint(flags, pltpu.VMEM),
            phase_table,
            fz1,
            fz2,
            yr1,
            yr2,
            zr1,
            zr2,
            pr_up,
            pr_dn,
            own,
        )

    in_specs = (
        P(None, ("groups", "wide"), "narrow", None),
        P(("groups", "wide"), "narrow", None),
        P(("groups", "wide"), "narrow", None),
        P(("groups", "wide"), "narrow", None),
        P(("groups", "wide"), "narrow", None),
        P(),
        P(None, ("groups", "wide"), "narrow", None),
    )
    out_specs = (
        P(None, ("groups", "wide"), "narrow", None),
        P(("groups", "wide"), "narrow", None),
        P(None, ("groups", "wide"), "narrow", None),
    )
    return jax.shard_map(
        per_device, mesh=mesh, in_specs=in_specs, out_specs=out_specs, check_vma=False
    )
```

```python
import jax
import jax.numpy as jnp
from jax import lax
from jax.experimental import pallas as pl
from jax.experimental.pallas import tpu as pltpu
from jax.sharding import PartitionSpec as P

lattice_dirs = [
    (0, 0, 0),
    (1, 0, 0),
    (-1, 0, 0),
    (0, 1, 0),
    (0, -1, 0),
    (0, 0, 1),
    (0, 0, -1),
    (1, 1, 0),
    (-1, -1, 0),
    (1, -1, 0),
    (-1, 1, 0),
    (1, 0, 1),
    (-1, 0, -1),
    (1, 0, -1),
    (-1, 0, 1),
    (0, 1, 1),
    (0, -1, -1),
    (0, 1, -1),
    (0, -1, 1),
]
opposite_dir = [0, 2, 1, 4, 3, 6, 5, 8, 7, 10, 9, 12, 11, 14, 13, 16, 15, 18, 17]
pairs = [(i, opposite_dir[i]) for i in range(1, 19) if i < opposite_dir[i]]
relax_time = 0.8
force_scale = 0.02
inlet_speed = 0.05
force_factor = 1.0 - 0.5 / relax_time

leave_yp = [3, 7, 10, 15, 17]
leave_ym = [4, 8, 9, 16, 18]
leave_zp = [5, 11, 14, 15, 18]
leave_zm = [6, 12, 13, 16, 17]

FACE = 10
GROUPS = 7
POT, SRC, COND, PH, MX, MY, MZ = range(GROUPS)
RIM = 4
CLOSED = -1e30
OPEN_ABOVE = -1e29
INNER_COST = pl.CostEstimate(flops=20000000000, bytes_accessed=12000000, transcendentals=0)
VMEM_LIMIT = 24 * 1024 * 1024

any_spec = pl.BlockSpec(memory_space=pl.ANY)
hbm_spec = pl.BlockSpec(memory_space=pltpu.HBM)
vmem_spec = pl.BlockSpec(memory_space=pltpu.VMEM)


def moments(f):
    d = {}
    rho = f[0]
    for i, j in pairs:
        rho = rho + (f[i] + f[j])
        d[i] = f[i] - f[j]
    mx = d[1] + d[7] + d[9] + d[11] + d[13]
    my = d[3] + d[7] - d[9] + d[15] + d[17]
    mz = d[5] + d[11] - d[13] + d[15] - d[17]
    return rho, mx, my, mz


def coefficients(rho, mom, force, fluid, inlet):
    inv = 1.0 / rho
    u = [(m + 0.5 * f) * inv for m, f in zip(mom, force)]
    u = [jnp.where(inlet, c, v) for c, v in zip((0.0, 0.0, -inlet_speed), u)]
    r = jnp.where(fluid, rho * (1.0 / (36.0 * relax_time)), 1.0 / 36.0)
    f = [jnp.where(fluid, v * (force_factor / 36.0), 0.0) for v in force]
    sq = u[0] * u[0] + u[1] * u[1] + u[2] * u[2]
    uf = u[0] * f[0] + u[1] * f[1] + u[2] * f[2]
    base = r * (1.0 - 1.5 * sq) - 3.0 * uf
    ru = [r * v for v in u]
    g = [4.5 * a + 9.0 * b for a, b in zip(ru, f)]
    h = [3.0 * (a + b) for a, b in zip(ru, f)]
    keep = jnp.where(fluid, 1.0 - 1.0 / relax_time, 0.0)
    return keep, base, u, g, h


def along(c, v):
    total = None
    for s, x in zip(c, v):
        if s == 0:
            continue
        if total is None:
            total = x if s > 0 else -x
        else:
            total = total + x if s > 0 else total - x
    return total


def post_pair(i, co):
    keep, base, u, g, h = co
    c = lattice_dirs[i]
    sym = base + along(c, u) * along(c, g)
    anti = along(c, h)
    if sum(abs(s) for s in c) == 1:
        return 2.0 * sym, 2.0 * anti
    return sym, anti


def post_one(i, f, co):
    keep = co[0]
    if i < opposite_dir[i]:
        sym, anti = post_pair(i, co)
        return keep * f + (sym + anti)
    sym, anti = post_pair(opposite_dir[i], co)
    return keep * f + (sym - anti)


def pick(cond, a, b):
    return jnp.where(cond, a, b)


def beyond_face(values, leave, force, there):
    flag = values[9]
    co = coefficients(values[5], values[6:9], force, flag < 0.5, (flag > 1.5) & (flag < 2.5))
    shut = (flag > 0.5) & (flag < 1.5)
    shut = shut | jnp.logical_not(there)
    return [(i, pick(shut, CLOSED, post_one(i, values[k], co))) for k, i in leave]


def lanes_to(x, shift):
    shift = shift % 128
    return x if shift == 0 else pltpu.roll(x, shift, 1)


def y_sections(nz):
    found, at = [], FACE * nz
    for rows in [RIM, RIM, 1, 1, 1, 1, 1] + [RIM] * 4:
        found.append((at, rows))
        at += rows
    return found, at, at + -at % 8


def pack_coarse(
    flags,
    pot_hbm,
    cond_hbm,
    ph_hbm,
    mag_hbm,
    tab_hbm,
    o_c1,
    o_c2,
    o_g,
    fbuf,
    zsc,
    pot,
    cond,
    ph,
    mag,
    tab,
    sems,
):
    nz, ny = flags.shape[0], flags.shape[1]
    kz, ky, kx = pot.shape
    coarse = [
        pltpu.make_async_copy(a, b, sems.at[2 + k])
        for k, (a, b) in enumerate(
            ((tab_hbm, tab), (ph_hbm, ph), (cond_hbm, cond), (pot_hbm, pot), (mag_hbm, mag))
        )
    ]
    copies = [
        pltpu.make_async_copy(flags.at[plane], fbuf.at[k], sems.at[k])
        for k, plane in enumerate((0, nz - 1))
    ]
    for c in coarse + copies:
        c.start()
    for c in coarse:
        c.wait()
    phase = ph[...]
    conductivity = cond[...]
    source = conductivity * jnp.where(
        phase == 0, tab[0, 0], jnp.where(phase == 1, tab[1, 0], tab[2, 0])
    )
    fields = [pot[...], source, conductivity, phase.astype(jnp.float32), mag[0], mag[1], mag[2]]
    blank = jnp.zeros((ky, 128 - kz * kx), jnp.float32)
    for g, field in enumerate(fields):
        row = jnp.concatenate([field[l] for l in range(kz)] + [blank], axis=1)
        o_g[g, 0:ky, :] = row
        if g <= SRC:
            for side in range(2):
                zsc[side, ny + ky * g : ny + ky * g + ky, :] = row
    for c in copies:
        c.wait()
    for side in range(2):
        zsc[side, 0:ny, :] = fbuf[side].astype(jnp.float32)
    up_z = 1 - lax.axis_index("wide") % 2
    o_c1[...] = zsc[up_z]
    o_c2[...] = zsc[1 - up_z]


def pack_y_faces(pops, flags, after, o_y, ybuf, fybuf, sems):
    nz, ny = pops.shape[1], pops.shape[2]
    copies = []
    for side, row in ((0, 0), (1, ny - 8)):
        rows = pl.ds(row, 8)
        copies.append(pltpu.make_async_copy(pops.at[:, :, rows, :], ybuf.at[side], sems.at[side]))
        copies.append(pltpu.make_async_copy(flags.at[:, rows, :], fybuf.at[side], sems.at[2 + side]))
    for c in copies:
        c.start()
    for c in copies:
        c.wait()
    for side, leave, row in ((0, leave_ym, 0), (1, leave_yp, 7)):
        for z in range(nz):
            f = [ybuf[side, i, z] for i in range(19)]
            values = [f[i] for i in leave] + list(moments(f))
            values.append(fybuf[side, z].astype(jnp.float32))
            for k, v in enumerate(values):
                o_y[side, k * nz + z : k * nz + z + 1, :] = v[row : row + 1]


def coarse_blocks(ny, ky, low, high, own):
    blocks = [own[g, 0:ky, :] for g in range(GROUPS)]
    for side in (low, high):
        blocks += [side[ny + ky * g : ny + ky * g + ky] for g in (POT, SRC)]
    return blocks


def pack_rows(ny, ky, nz, zr1, zr2, own, fine, o_y1, o_y2, ysc):
    even = lax.axis_index("wide") % 2 == 0
    low = pick(even, zr2[...], zr1[...])
    high = pick(even, zr1[...], zr2[...])
    sections, used, total = y_sections(nz)
    blocks = coarse_blocks(ny, ky, low, high, own)
    for side in range(2):
        ysc[side, 0 : FACE * nz, :] = fine[side]
        for (at, rows), v in zip(sections, blocks):
            ysc[side, at : at + rows, :] = v[ky - rows : ky] if side else v[0:rows]
        if used < total:
            ysc[side, used:total, :] = jnp.zeros((total - used, 128), jnp.float32)
    up_y = 1 - lax.axis_index("narrow") % 2
    o_y1[...] = ysc[up_y]
    o_y2[...] = ysc[1 - up_y]


def collide_plane(z, to, pops, flags, fu, post):
    ny = flags.shape[1]
    l = z // 4
    for b in range(ny // 8):
        rows = slice(8 * b, 8 * b + 8)
        out = slice(8 + 8 * b, 16 + 8 * b)
        f = [pops[i, z, rows, :] for i in range(19)]
        flag = flags[z, rows, :]
        force = [fu[l, a, rows, :] for a in range(3)]
        rho, mom_x, mom_y, mom_z = moments(f)
        wall = flag == 1
        co = coefficients(rho, (mom_x, mom_y, mom_z), force, flag == 0, flag == 2)
        keep = co[0]
        post[0, to, out, :] = pick(wall, CLOSED, keep * f[0] + 12.0 * co[1])
        for i, j in pairs:
            sym, anti = post_pair(i, co)
            post[i, to, out, :] = pick(wall, CLOSED, keep * f[i] + (sym + anti))
            post[j, to, out, :] = pick(wall, CLOSED, keep * f[j] + (sym - anti))


def pass_plane(z, pops, flags, here, source, put):
    ny, nx = flags.shape[1:]
    lane8 = lax.broadcasted_iota(jnp.int32, (8, 128), 1)
    not_first = lane8 > 0
    not_last = lane8 < nx - 1
    for b in range(ny // 8):
        rows = slice(8 * b, 8 * b + 8)
        out = slice(8 + 8 * b, 16 + 8 * b)
        wall = flags[z, rows, :] == 1
        for i in range(19):
            cx, cy, cz = lattice_dirs[i]
            own = here(opposite_dir[i], out)
            if i > 0:
                v = source(i, cz, slice(8 + 8 * b - cy, 16 + 8 * b - cy))
                if cx != 0:
                    v = pltpu.roll(v, cx % nx, 1)
                ok = v > OPEN_ABOVE
                if cx == 1:
                    ok = ok & not_first
                if cx == -1:
                    ok = ok & not_last
                own = pick(ok, v, own)
            put(i, rows, pick(wall, pops[i, z, rows, :], own))


def face_kernel(
    W,
    N,
    pops,
    flags,
    tab_hbm,
    yr1,
    yr2,
    zr1,
    zr2,
    own,
    o_pot,
    o_lor,
    o_f1,
    o_f2,
    post,
    o_yh,
    fu,
    ext,
    fc,
    zsc,
    tab,
    sem_tab,
):
    nz, ny, nx = flags.shape
    kz, ky, kx = o_pot.shape
    wi, ni = lax.axis_index("wide"), lax.axis_index("narrow")
    tcopy = pltpu.make_async_copy(tab_hbm, tab, sem_tab)
    tcopy.start()
    even_z = wi % 2 == 0
    even_y = ni % 2 == 0
    has_low_y, has_high_y = ni > 0, ni < N - 1

    z_lo = pick(even_z, zr2[...], zr1[...])
    z_hi = pick(even_z, zr1[...], zr2[...])
    y_lo = pick(even_y, yr2[...], yr1[...])
    y_hi = pick(even_y, yr1[...], yr2[...])
    sections = y_sections(nz)[0]
    blocks = coarse_blocks(ny, ky, z_lo, z_hi, own)
    blank = jnp.zeros((RIM, 128), jnp.float32)
    for k, ((at, rows), v) in enumerate(zip(sections, blocks)):
        if rows < RIM:
            ext[k, 0:RIM, :] = blank
            ext[k, RIM + ky : 2 * RIM + ky, :] = blank
        ext[k, RIM - rows : RIM, :] = y_lo[at : at + rows]
        ext[k, RIM : RIM + ky, :] = v
        ext[k, RIM + ky : RIM + ky + rows, :] = y_hi[at : at + rows]
        ext[k, 2 * RIM + ky : 24, :] = jnp.zeros((24 - 2 * RIM - ky, 128), jnp.float32)
    below, above = GROUPS, GROUPS + 2

    shape = (24, 128)
    lane = lax.broadcasted_iota(jnp.int32, shape, 1)
    row = lax.broadcasted_iota(jnp.int32, shape, 0)
    y_at = ni * ky + row - RIM
    y_in = (y_at >= 0) & (y_at < ky * N)
    layer = lane // kx
    x_at = lane - layer * kx

    def inside(first):
        z_at = wi * kz + first + layer
        return y_in & (z_at >= 0) & (z_at < kz * W) & (layer < kz)

    inner = [inside(-kz), inside(0), inside(kz)]

    def three(g):
        return [ext[below + g], ext[g], ext[above + g]]

    zero = jnp.zeros(shape, jnp.float32)
    field = [pick(m, v, 0.0) for m, v in zip(inner, three(POT))]
    source = three(SRC)
    last = (kz - 1) * kx

    def next_z(here, above):
        return pick(lane < last, lanes_to(here, -kx), lanes_to(above, last))

    def prev_z(here, below):
        return pick(lane >= kx, lanes_to(here, kx), lanes_to(below, -last))

    def next_x(v):
        return pick(x_at == kx - 1, 0.0, lanes_to(v, -1))

    def prev_x(v):
        return pick(x_at == 0, 0.0, lanes_to(v, 1))

    def next_y(v):
        return pltpu.roll(v, 23, 0)

    def prev_y(v):
        return pltpu.roll(v, 1, 0)

    def sweep(values, lower, upper):
        chain = [lower] + values + [upper]
        new = []
        for k in range(3):
            v = values[k]
            total = next_z(v, chain[k + 2]) + prev_z(v, chain[k])
            total = total + next_y(v) + prev_y(v)
            total = total + next_x(v) + prev_x(v)
            new.append(pick(inner[k], (total + source[k]) / 6.0, 0.0))
        return new

    field = sweep(field, zero, zero)
    field = sweep(field, zero, zero)

    tcopy.wait()
    v = field[1]
    grad = (
        (next_x(v) - prev_x(v)) * 0.5,
        (next_y(v) - prev_y(v)) * 0.5,
        (next_z(v, field[2]) - prev_z(v, field[0])) * 0.5,
    )
    phase = ext[PH]
    cur = []
    for a in range(3):
        applied = pick(phase < 0.5, tab[0, 1 + a], pick(phase < 1.5, tab[1, 1 + a], tab[2, 1 + a]))
        cur.append(ext[COND] * (applied - grad[a]))
    lorentz = [
        cur[1] * ext[MZ] - cur[2] * ext[MY],
        cur[2] * ext[MX] - cur[0] * ext[MZ],
        cur[0] * ext[MY] - cur[1] * ext[MX],
    ]
    for l in range(kz):
        o_pot[l] = lanes_to(field[1], -kx * l)[RIM : RIM + ky, 0:kx]
        for a in range(3):
            o_lor[a, l] = lanes_to(lorentz[a], -kx * l)[RIM : RIM + ky, 0:kx]

    src = lax.broadcasted_iota(jnp.int32, (128, 128), 0)
    dst = lax.broadcasted_iota(jnp.int32, (128, 128), 1) // (nx // kx)

    def widened(stack, l):
        choose = jnp.where(src == kx * l + dst, 1.0, 0.0)
        return lax.dot_general(
            stack,
            choose,
            (((1,), (0,)), ((), ())),
            precision=lax.Precision.HIGHEST,
            preferred_element_type=jnp.float32,
        )

    stack = jnp.concatenate([v * force_scale for v in lorentz], axis=0)
    wide = [widened(stack, l) for l in range(kz)]
    sub = lax.broadcasted_iota(jnp.int32, (8, 128), 0)
    for l in range(kz):
        for a in range(3):
            fc[l, a] = wide[l][24 * a : 24 * a + 24]
    for l in range(kz):
        for a in range(3):
            for b in range(ny // 8):
                first = jnp.broadcast_to(fc[l, a, pl.ds(RIM + 2 * b, 1), :], (8, 128))
                second = jnp.broadcast_to(fc[l, a, pl.ds(RIM + 2 * b + 1, 1), :], (8, 128))
                fu[l, a, 8 * b : 8 * b + 8, :] = pick(sub < 4, first, second)

    zrow = lax.broadcasted_iota(jnp.int32, (nz, 128), 0)
    for low, leave, frow, at, there in (
        (True, leave_yp, RIM - 1, 7, has_low_y),
        (False, leave_ym, RIM + ky, 8 + ny, has_high_y),
    ):
        side = y_lo if low else y_hi
        values = [side[nz * k : nz * k + nz] for k in range(FACE)]
        force = []
        for a in range(3):
            rows = [jnp.broadcast_to(fc[l, a, frow : frow + 1, :], (nz, 128)) for l in range(kz)]
            v = rows[kz - 1]
            for l in range(kz - 2, -1, -1):
                v = pick(zrow < 4 * (l + 1), rows[l], v)
            force.append(v)
        there_b = jnp.broadcast_to(there, (nz, 128))
        for k, (i, v) in enumerate(beyond_face(values, list(enumerate(leave)), force, there_b)):
            o_yh[0 if low else 1, k, 0:nz, :] = v
            for to, z in enumerate((0, nz - 1)):
                post[i, to, at : at + 1, :] = v[z : z + 1]

    collide_plane(0, 0, pops, flags, fu, post)
    collide_plane(nz - 1, 1, pops, flags, fu, post)
    for side, leave, edges in ((0, leave_zm, (17, 16)), (1, leave_zp, (15, 18))):
        for k, i in enumerate(leave):
            zsc[side, ny * k : ny * k + ny, :] = post[i, side, 8 : 8 + ny, :]
        at = 5 * ny
        z = side * (nz - 1)
        for y_side, (i, rows) in enumerate(zip(edges, (y_lo, y_hi))):
            yrow = 8 + ny if y_side else 7
            zsc[side, at + y_side : at + y_side + 1, :] = post[i, side, yrow : yrow + 1, :]
            row = 9 * nz + z
            zsc[side, at + 2 + y_side : at + 3 + y_side, :] = rows[row : row + 1]
        zsc[side, at + 4 : at + 8, :] = jnp.zeros((4, 128), jnp.float32)
    up_z = 1 - wi % 2
    o_f1[...] = zsc[up_z]
    o_f2[...] = zsc[1 - up_z]


def inner_kernel(pops, flags, faces, yh, fu, o_pops, o_near, obuf, post, sem_out):
    nz, ny, nx = flags.shape
    for i in range(19):
        post[i, 0] = faces[i, 0]
        post[i, nz - 1] = faces[i, 1]
    for side, leave, at in ((0, leave_yp, 7), (1, leave_ym, 8 + ny)):
        for k, i in enumerate(leave):
            rows = yh[side, k]
            for z in range(1, nz - 1):
                post[i, z, at : at + 1, :] = rows[z : z + 1]

    def passing(z):
        def put(i, rows, v):
            obuf[i, z, rows, :] = v

        pass_plane(
            z,
            pops,
            flags,
            lambda i, rows: post[i, z, rows, :],
            lambda i, cz, rows: post[i, z - cz, rows, :],
            put,
        )
        pltpu.make_async_copy(obuf.at[:, z], o_pops.at[:, z], sem_out.at[z]).start()

    collide_plane(1, 1, pops, flags, fu, post)

    def plane(z, carry):
        collide_plane(z + 1, z + 1, pops, flags, fu, post)
        passing(z)
        return carry

    lax.fori_loop(1, nz - 2, plane, 0)
    passing(nz - 2)
    for i in range(19):
        o_near[i, 0] = post[i, 1]
        o_near[i, 1] = post[i, nz - 2]

    def drain(z, carry):
        pltpu.make_async_copy(obuf.at[:, z], o_pops.at[:, z], sem_out.at[z]).wait()
        return carry

    lax.fori_loop(1, nz - 1, drain, 0)


def outer_kernel(
    W, pops, flags, faces, near, fz1, fz2, zr1, zr2, half, o_pops, obuf, halo, sem_out
):
    nz, ny, nx = flags.shape
    wi = lax.axis_index("wide")
    even_z = wi % 2 == 0
    for side, leave, edges, there in (
        (0, leave_zp, (15, 18), wi > 0),
        (1, leave_zm, (17, 16), wi < W - 1),
    ):
        f_odd, f_even = (fz2, fz1) if side else (fz1, fz2)
        c_odd, c_even = (zr2, zr1) if side else (zr1, zr2)
        gone = jnp.broadcast_to(jnp.logical_not(there), (8, 128))
        for b in range(ny // 8):
            rows = slice(8 * b, 8 * b + 8)
            flag = pick(even_z, c_even[rows, :], c_odd[rows, :])
            shut = ((flag > 0.5) & (flag < 1.5)) | gone
            for k in range(5):
                at = slice(ny * k + 8 * b, ny * k + 8 * b + 8)
                v = pick(even_z, f_even[at, :], f_odd[at, :])
                halo[side, k, 8 + 8 * b : 16 + 8 * b, :] = pick(shut, CLOSED, v)
        at = slice(5 * ny, 5 * ny + 8)
        v = pick(even_z, f_even[at, :], f_odd[at, :])
        for y_side, i in enumerate(edges):
            flag = v[2 + y_side : 3 + y_side]
            shut = ((flag > 0.5) & (flag < 1.5)) | gone[0:1]
            yrow = 8 + ny if y_side else 7
            k = leave.index(i)
            edge = pick(shut, CLOSED, v[y_side : y_side + 1])
            halo[side, k, yrow : yrow + 1, :] = edge
    copies = []
    for side, z, leave in ((0, 0, leave_zp), (1, nz - 1, leave_zm)):

        def source(i, cz, rows, side=side, leave=leave):
            if cz == 0:
                return faces[i, side, rows, :]
            if i in leave:
                return halo[side, leave.index(i), rows, :]
            return near[i, side, rows, :]

        def put(i, rows, v, side=side):
            obuf[i, side, rows, :] = v

        pass_plane(z, pops, flags, lambda i, rows: faces[i, side, rows, :], source, put)
        copies.append(pltpu.make_async_copy(obuf.at[:, side], o_pops.at[:, z], sem_out.at[side]))
        copies[-1].start()
    for c in copies:
        c.wait()


def pair_first(size):
    return [(i, i ^ 1) for i in range(size)]


def pair_second(size, groups):
    found = []
    for g in range(groups):
        for i in range(size):
            j = i + 1 if i % 2 else i - 1
            if 0 <= j < size:
                found.append((g * size + i, g * size + j))
            elif g ^ 1 < groups:
                found.append((g * size + i, (g ^ 1) * size + i))
    return found


def solution(mesh):
    G, W, N = mesh.shape["groups"], mesh.shape["wide"], mesh.shape["narrow"]

    def per_device(populations, flags, potential, conductivity, coil_phase, phase_table, magnetic):
        f32 = jnp.float32
        nz, ny, nx = flags.shape
        kz, ky, kx = potential.shape
        zrows = ny + 2 * ky
        yrows = y_sections(nz)[2]
        frows = 5 * ny + 8
        params = pltpu.CompilerParams(vmem_limit_bytes=VMEM_LIMIT)
        shape = jax.ShapeDtypeStruct

        def in_hbm(*xs):
            return [pltpu.with_memory_space_constraint(x, pltpu.HBM) for x in xs]

        c1, c2, own = pl.pallas_call(
            pack_coarse,
            name="pack_coarse",
            out_shape=(
                shape((zrows, nx), f32),
                shape((zrows, nx), f32),
                shape((GROUPS, 16, nx), f32),
            ),
            in_specs=[hbm_spec] * 6,
            out_specs=[vmem_spec] * 3,
            scratch_shapes=[
                pltpu.VMEM((2, ny, nx), jnp.int32),
                pltpu.VMEM((2, zrows, nx), f32),
                pltpu.VMEM(potential.shape, f32),
                pltpu.VMEM(conductivity.shape, f32),
                pltpu.VMEM(coil_phase.shape, jnp.int32),
                pltpu.VMEM(magnetic.shape, f32),
                pltpu.SMEM(phase_table.shape, f32),
                pltpu.SemaphoreType.DMA((7,)),
            ],
            compiler_params=params,
        )(*in_hbm(flags, potential, conductivity, coil_phase, magnetic, phase_table))
        zr1 = lax.ppermute(c1, "wide", pair_first(W))
        zr2 = lax.ppermute(c2, ("groups", "wide"), pair_second(W, G))
        fine = pl.pallas_call(
            pack_y_faces,
            name="pack_y_faces",
            out_shape=shape((2, FACE * nz, nx), f32),
            in_specs=[hbm_spec] * 2 + [any_spec],
            out_specs=vmem_spec,
            scratch_shapes=[
                pltpu.VMEM((2, 19, nz, 8, nx), f32),
                pltpu.VMEM((2, nz, 8, nx), jnp.int32),
                pltpu.SemaphoreType.DMA((4,)),
            ],
            compiler_params=params,
        )(*in_hbm(populations, flags), own)
        y1, y2 = pl.pallas_call(
            lambda *refs: pack_rows(ny, ky, nz, *refs),
            name="pack_rows",
            out_shape=(shape((yrows, nx), f32), shape((yrows, nx), f32)),
            in_specs=[vmem_spec] * 4,
            out_specs=[vmem_spec] * 2,
            scratch_shapes=[pltpu.VMEM((2, yrows, nx), f32)],
            compiler_params=params,
        )(zr1, zr2, own, fine)
        yr1 = lax.ppermute(y1, "narrow", pair_first(N))
        yr2 = lax.ppermute(y2, ("groups", "narrow"), pair_second(N, G))
        pops_near = pltpu.with_memory_space_constraint(populations, pltpu.VMEM)
        flags_near = pltpu.with_memory_space_constraint(flags, pltpu.VMEM)
        pot_out, lorentz, f1, f2, faces, yh, force = pl.pallas_call(
            lambda *refs: face_kernel(W, N, *refs),
            name="faces",
            out_shape=(
                shape(potential.shape, f32),
                shape(magnetic.shape, f32),
                shape((frows, nx), f32),
                shape((frows, nx), f32),
                shape((19, 2, ny + 16, nx), f32),
                shape((2, 5, 16, nx), f32),
                shape((kz, 3, ny, nx), f32),
            ),
            in_specs=[vmem_spec] * 2 + [any_spec] + [vmem_spec] * 5,
            out_specs=[vmem_spec] * 7,
            scratch_shapes=[
                pltpu.VMEM((GROUPS + 4, 24, nx), f32),
                pltpu.VMEM((kz, 3, 24, nx), f32),
                pltpu.VMEM((2, frows, nx), f32),
                pltpu.SMEM(phase_table.shape, f32),
                pltpu.SemaphoreType.DMA,
            ],
            compiler_params=params,
        )(pops_near, flags_near, phase_table, yr1, yr2, zr1, zr2, own)
        fz1 = lax.ppermute(f1, "wide", pair_first(W))
        fz2 = lax.ppermute(f2, ("groups", "wide"), pair_second(W, G))
        half, near = pl.pallas_call(
            inner_kernel,
            name="inner",
            out_shape=(shape(populations.shape, f32), shape((19, 2, ny + 16, nx), f32)),
            in_specs=[vmem_spec] * 5,
            out_specs=[hbm_spec, vmem_spec],
            scratch_shapes=[
                pltpu.VMEM(populations.shape, f32),
                pltpu.VMEM((19, nz, ny + 16, nx), f32),
                pltpu.SemaphoreType.DMA((nz,)),
            ],
            compiler_params=params,
            cost_estimate=INNER_COST,
        )(pops_near, flags_near, faces, yh, force)
        passed = pl.pallas_call(
            lambda *refs: outer_kernel(W, *refs),
            name="outer",
            out_shape=shape(populations.shape, f32),
            in_specs=[vmem_spec] * 8 + [hbm_spec],
            out_specs=hbm_spec,
            input_output_aliases={8: 0},
            scratch_shapes=[
                pltpu.VMEM((19, 2, ny, nx), f32),
                pltpu.VMEM((2, 5, ny + 16, nx), f32),
                pltpu.SemaphoreType.DMA((2,)),
            ],
            compiler_params=params,
        )(pops_near, flags_near, faces, near, fz1, fz2, zr1, zr2, half)
        return passed, pot_out, lorentz

    in_specs = (
        P(None, ("groups", "wide"), "narrow", None),
        P(("groups", "wide"), "narrow", None),
        P(("groups", "wide"), "narrow", None),
        P(("groups", "wide"), "narrow", None),
        P(("groups", "wide"), "narrow", None),
        P(),
        P(None, ("groups", "wide"), "narrow", None),
    )
    out_specs = (
        P(None, ("groups", "wide"), "narrow", None),
        P(("groups", "wide"), "narrow", None),
        P(None, ("groups", "wide"), "narrow", None),
    )
    return jax.shard_map(
        per_device, mesh=mesh, in_specs=in_specs, out_specs=out_specs, check_vma=False
    )
```

```python
import jax
import jax.numpy as jnp
from jax import lax
from jax.experimental import pallas as pl
from jax.experimental.pallas import tpu as pltpu
from jax.sharding import PartitionSpec as P

lattice_dirs = [
    (0, 0, 0),
    (1, 0, 0),
    (-1, 0, 0),
    (0, 1, 0),
    (0, -1, 0),
    (0, 0, 1),
    (0, 0, -1),
    (1, 1, 0),
    (-1, -1, 0),
    (1, -1, 0),
    (-1, 1, 0),
    (1, 0, 1),
    (-1, 0, -1),
    (1, 0, -1),
    (-1, 0, 1),
    (0, 1, 1),
    (0, -1, -1),
    (0, 1, -1),
    (0, -1, 1),
]
opposite_dir = [0, 2, 1, 4, 3, 6, 5, 8, 7, 10, 9, 12, 11, 14, 13, 16, 15, 18, 17]
pairs = [(i, opposite_dir[i]) for i in range(1, 19) if i < opposite_dir[i]]
relax_time = 0.8
force_scale = 0.02
inlet_speed = 0.05
force_factor = 1.0 - 0.5 / relax_time
PUSH = 6.0 * force_factor / 36.0

leave_yp = [3, 7, 10, 15, 17]
leave_ym = [4, 8, 9, 16, 18]
leave_zp = [5, 11, 14, 15, 18]
leave_zm = [6, 12, 13, 16, 17]

FACE = 10
GROUPS = 9
POT, SRC, COND, MX, MY, MZ, AX, AY, AZ = range(GROUPS)
RIM = 4
CLOSED = -1e30
OPEN_ABOVE = -1e29
INNER_COST = pl.CostEstimate(flops=20000000000, bytes_accessed=12000000, transcendentals=0)
VMEM_LIMIT = 24 * 1024 * 1024

any_spec = pl.BlockSpec(memory_space=pl.ANY)
hbm_spec = pl.BlockSpec(memory_space=pltpu.HBM)
vmem_spec = pl.BlockSpec(memory_space=pltpu.VMEM)


def pick(cond, a, b):
    return jnp.where(cond, a, b)


def moments(f):
    d = {}
    rho = f[0]
    for i, j in pairs:
        rho = rho + (f[i] + f[j])
        d[i] = f[i] - f[j]
    mx = d[1] + d[7] + d[9] + d[11] + d[13]
    my = d[3] + d[7] - d[9] + d[15] + d[17]
    mz = d[5] + d[11] - d[13] + d[15] - d[17]
    return rho, mx, my, mz


def coefficients(rho, mom, half, push, fluid, inlet, shut):
    inv = 1.5 / rho
    still = inlet | shut
    b = [pick(still, 0.0, (m + f) * inv) for m, f in zip(mom[:2], half[:2])]
    b.append(pick(still, pick(inlet, -1.5 * inlet_speed, 0.0), (mom[2] + half[2]) * inv))
    r = pick(fluid, rho * (1.0 / (36.0 * relax_time)), pick(shut, CLOSED, 1.0 / 36.0))
    p = [pick(fluid, v, 0.0) for v in push]
    r2 = r + r
    h = [r2 * v + w for v, w in zip(b, p)]
    e = [v + w for v, w in zip(h, p)]
    base = r - (b[0] * e[0] + b[1] * e[1] + b[2] * e[2]) * (1.0 / 3.0)
    keep = pick(fluid, 1.0 - 1.0 / relax_time, 0.0)
    return keep, base, b, e, h


def along(c, v):
    total = None
    for s, x in zip(c, v):
        if s == 0:
            continue
        if total is None:
            total = x if s > 0 else -x
        else:
            total = total + x if s > 0 else total - x
    return total


def post_pair(i, co):
    _, base, b, e, h = co
    c = lattice_dirs[i]
    sym = base + along(c, b) * along(c, e)
    anti = along(c, h)
    if sum(abs(s) for s in c) == 1:
        return sym + sym, anti + anti
    return sym, anti


def post_one(i, f, co):
    keep = co[0]
    if i < opposite_dir[i]:
        sym, anti = post_pair(i, co)
        return keep * f + (sym + anti)
    sym, anti = post_pair(opposite_dir[i], co)
    return keep * f + (sym - anti)


def beyond_face(values, leave, half, there):
    flag = values[9]
    shut = (flag > 0.5) & (flag < 1.5)
    shut = shut | jnp.logical_not(there)
    fluid = (flag < 0.5) & there
    inlet = (flag > 1.5) & (flag < 2.5) & there
    push = [v * PUSH for v in half]
    co = coefficients(values[5], values[6:9], half, push, fluid, inlet, shut)
    return [(i, post_one(i, values[k], co)) for k, i in leave]


def lanes_to(x, shift):
    shift = shift % 128
    return x if shift == 0 else pltpu.roll(x, shift, 1)


def y_sections(nz):
    found, at = [], FACE * nz
    for rows in [RIM] * 2 + [1] * (GROUPS - 2) + [RIM] * 4:
        found.append((at, rows))
        at += rows
    return found, at, at + -at % 8


def pack_coarse(
    pot_hbm,
    cond_hbm,
    ph_hbm,
    mag_hbm,
    tab_hbm,
    o_c1,
    o_c2,
    o_g,
    pot,
    cond,
    ph,
    mag,
    tab,
    sems,
):
    kz, ky, kx = pot.shape
    coarse = [
        pltpu.make_async_copy(a, b, sems.at[k])
        for k, (a, b) in enumerate(
            ((tab_hbm, tab), (ph_hbm, ph), (cond_hbm, cond), (pot_hbm, pot), (mag_hbm, mag))
        )
    ]
    for c in coarse:
        c.start()
    for c in coarse:
        c.wait()
    phase = ph[...]
    conductivity = cond[...]
    column = [
        pick(phase == 0, tab[0, k], pick(phase == 1, tab[1, k], tab[2, k])) for k in range(4)
    ]
    fields = [pot[...], conductivity * column[0], conductivity, mag[0], mag[1], mag[2]]
    fields += column[1:]
    blank = jnp.zeros((ky, 128 - kz * kx), jnp.float32)
    for g, field in enumerate(fields):
        row = jnp.concatenate([field[l] for l in range(kz)] + [blank], axis=1)
        o_g[g, 0:ky, :] = row
        if g <= SRC:
            o_c1[ky * g : ky * g + ky, :] = row
            o_c2[ky * g : ky * g + ky, :] = row


def pack_y_faces(pops, flags, after, o_y, ybuf, fbuf, sems):
    nz, ny = pops.shape[1], pops.shape[2]
    copies = []
    for side, row in ((0, 0), (1, ny - 1)):
        copies.append(pltpu.make_async_copy(pops.at[:, :, row, :], ybuf.at[side], sems.at[side]))
        copies.append(pltpu.make_async_copy(flags.at[:, row, :], fbuf.at[side], sems.at[2 + side]))
    for c in copies:
        c.start()
    for c in copies:
        c.wait()
    for side, leave in ((0, leave_ym), (1, leave_yp)):
        f = [ybuf[side, i] for i in range(19)]
        values = [f[i] for i in leave] + list(moments(f))
        values.append(fbuf[side].astype(jnp.float32))
        for k, v in enumerate(values):
            o_y[side, k * nz : k * nz + nz, :] = v


def coarse_blocks(ky, low, high, own):
    blocks = [own[g, 0:ky, :] for g in range(GROUPS)]
    for side in (low, high):
        blocks += [side[ky * g : ky * g + ky] for g in (POT, SRC)]
    return blocks


def pack_rows(ky, nz, zr1, zr2, own, fine, o_y1, o_y2, ysc):
    even = lax.axis_index("wide") % 2 == 0
    low = pick(even, zr2[...], zr1[...])
    high = pick(even, zr1[...], zr2[...])
    sections, used, total = y_sections(nz)
    blocks = coarse_blocks(ky, low, high, own)
    for side in range(2):
        ysc[side, 0 : FACE * nz, :] = fine[side]
        for (at, rows), v in zip(sections, blocks):
            ysc[side, at : at + rows, :] = v[ky - rows : ky] if side else v[0:rows]
        if used < total:
            ysc[side, used:total, :] = jnp.zeros((total - used, 128), jnp.float32)
    up_y = 1 - lax.axis_index("narrow") % 2
    o_y1[...] = ysc[up_y]
    o_y2[...] = ysc[1 - up_y]


def collide_plane(z, to, pops, flags, fu, post):
    ny = flags.shape[1]
    l = z // 4
    for b in range(ny // 8):
        rows = slice(8 * b, 8 * b + 8)
        out = slice(8 + 8 * b, 16 + 8 * b)
        f = [pops[i, z, rows, :] for i in range(19)]
        flag = flags[z, rows, :]
        half = [fu[l, a, rows, :] for a in range(3)]
        push = [fu[l, 3 + a, rows, :] for a in range(3)]
        rho, mom_x, mom_y, mom_z = moments(f)
        co = coefficients(
            rho, (mom_x, mom_y, mom_z), half, push, flag == 0, flag == 2, flag == 1
        )
        keep = co[0]
        post[0, to, out, :] = keep * f[0] + 12.0 * co[1]
        for i, j in pairs:
            sym, anti = post_pair(i, co)
            post[i, to, out, :] = keep * f[i] + (sym + anti)
            post[j, to, out, :] = keep * f[j] + (sym - anti)


def pass_plane(z, pops, flags, here, source, put):
    ny, nx = flags.shape[1:]
    lane8 = lax.broadcasted_iota(jnp.int32, (8, 128), 1)
    not_first = lane8 > 0
    not_last = lane8 < nx - 1
    for b in range(ny // 8):
        rows = slice(8 * b, 8 * b + 8)
        out = slice(8 + 8 * b, 16 + 8 * b)
        wall = flags[z, rows, :] == 1
        for i in range(19):
            cx, cy, cz = lattice_dirs[i]
            own = here(opposite_dir[i], out)
            if i > 0:
                v = source(i, cz, slice(8 + 8 * b - cy, 16 + 8 * b - cy))
                if cx != 0:
                    v = pltpu.roll(v, cx % nx, 1)
                ok = v > OPEN_ABOVE
                if cx == 1:
                    ok = ok & not_first
                if cx == -1:
                    ok = ok & not_last
                own = pick(ok, v, own)
            put(i, rows, pick(wall, pops[i, z, rows, :], own))


def face_kernel(
    W,
    N,
    pops,
    flags,
    yr1,
    yr2,
    zr1,
    zr2,
    own,
    o_pot,
    o_lor,
    o_f1,
    o_f2,
    post,
    o_yh,
    fu,
    ext,
    fc,
    zsc,
):
    nz, ny, nx = flags.shape
    kz, ky, kx = o_pot.shape
    wi, ni = lax.axis_index("wide"), lax.axis_index("narrow")
    even_z = wi % 2 == 0
    even_y = ni % 2 == 0
    has_low_y, has_high_y = ni > 0, ni < N - 1

    z_lo = pick(even_z, zr2[...], zr1[...])
    z_hi = pick(even_z, zr1[...], zr2[...])
    y_lo = pick(even_y, yr2[...], yr1[...])
    y_hi = pick(even_y, yr1[...], yr2[...])
    sections = y_sections(nz)[0]
    blocks = coarse_blocks(ky, z_lo, z_hi, own)
    blank = jnp.zeros((RIM, 128), jnp.float32)
    for k, ((at, rows), v) in enumerate(zip(sections, blocks)):
        if rows < RIM:
            ext[k, 0:RIM, :] = blank
            ext[k, RIM + ky : 2 * RIM + ky, :] = blank
        ext[k, RIM - rows : RIM, :] = y_lo[at : at + rows]
        ext[k, RIM : RIM + ky, :] = v
        ext[k, RIM + ky : RIM + ky + rows, :] = y_hi[at : at + rows]
        ext[k, 2 * RIM + ky : 24, :] = jnp.zeros((24 - 2 * RIM - ky, 128), jnp.float32)
    below, above = GROUPS, GROUPS + 2

    shape = (24, 128)
    lane = lax.broadcasted_iota(jnp.int32, shape, 1)
    row = lax.broadcasted_iota(jnp.int32, shape, 0)
    y_at = ni * ky + row - RIM
    y_in = (y_at >= 0) & (y_at < ky * N)
    layer = lane // kx
    x_at = lane - layer * kx

    def inside(first):
        z_at = wi * kz + first + layer
        return y_in & (z_at >= 0) & (z_at < kz * W) & (layer < kz)

    inner = [inside(-kz), inside(0), inside(kz)]

    def three(g):
        return [ext[below + g], ext[g], ext[above + g]]

    zero = jnp.zeros(shape, jnp.float32)
    field = [pick(m, v, 0.0) for m, v in zip(inner, three(POT))]
    source = three(SRC)
    last = (kz - 1) * kx

    def next_z(here, above):
        return pick(lane < last, lanes_to(here, -kx), lanes_to(above, last))

    def prev_z(here, below):
        return pick(lane >= kx, lanes_to(here, kx), lanes_to(below, -last))

    def next_x(v):
        return pick(x_at == kx - 1, 0.0, lanes_to(v, -1))

    def prev_x(v):
        return pick(x_at == 0, 0.0, lanes_to(v, 1))

    def next_y(v):
        return pltpu.roll(v, 23, 0)

    def prev_y(v):
        return pltpu.roll(v, 1, 0)

    def sweep(values, lower, upper):
        chain = [lower] + values + [upper]
        new = []
        for k in range(3):
            v = values[k]
            total = next_z(v, chain[k + 2]) + prev_z(v, chain[k])
            total = total + next_y(v) + prev_y(v)
            total = total + next_x(v) + prev_x(v)
            new.append(pick(inner[k], (total + source[k]) / 6.0, 0.0))
        return new

    field = sweep(field, zero, zero)
    field = sweep(field, zero, zero)

    v = field[1]
    grad = (
        (next_x(v) - prev_x(v)) * 0.5,
        (next_y(v) - prev_y(v)) * 0.5,
        (next_z(v, field[2]) - prev_z(v, field[0])) * 0.5,
    )
    cur = [ext[COND] * (ext[AX + a] - grad[a]) for a in range(3)]
    lorentz = [
        cur[1] * ext[MZ] - cur[2] * ext[MY],
        cur[2] * ext[MX] - cur[0] * ext[MZ],
        cur[0] * ext[MY] - cur[1] * ext[MX],
    ]
    for l in range(kz):
        o_pot[l] = lanes_to(field[1], -kx * l)[RIM : RIM + ky, 0:kx]
        for a in range(3):
            o_lor[a, l] = lanes_to(lorentz[a], -kx * l)[RIM : RIM + ky, 0:kx]

    src = lax.broadcasted_iota(jnp.int32, (128, 128), 0)
    dst = lax.broadcasted_iota(jnp.int32, (128, 128), 1) // (nx // kx)

    def widened(stack, l):
        choose = jnp.where(src == kx * l + dst, 1.0, 0.0)
        return lax.dot_general(
            stack,
            choose,
            (((1,), (0,)), ((), ())),
            precision=lax.Precision.HIGHEST,
            preferred_element_type=jnp.float32,
        )

    stack = jnp.concatenate([v * (0.5 * force_scale) for v in lorentz], axis=0)
    wide = [widened(stack, l) for l in range(kz)]
    sub = lax.broadcasted_iota(jnp.int32, (8, 128), 0)
    for l in range(kz):
        for a in range(3):
            fc[l, a] = wide[l][24 * a : 24 * a + 24]
    for l in range(kz):
        for a in range(3):
            for b in range(ny // 8):
                first = jnp.broadcast_to(fc[l, a, pl.ds(RIM + 2 * b, 1), :], (8, 128))
                second = jnp.broadcast_to(fc[l, a, pl.ds(RIM + 2 * b + 1, 1), :], (8, 128))
                half = pick(sub < 4, first, second)
                fu[l, a, 8 * b : 8 * b + 8, :] = half
                fu[l, 3 + a, 8 * b : 8 * b + 8, :] = half * PUSH

    zrow = lax.broadcasted_iota(jnp.int32, (nz, 128), 0)
    for low, leave, frow, at, there in (
        (True, leave_yp, RIM - 1, 7, has_low_y),
        (False, leave_ym, RIM + ky, 8 + ny, has_high_y),
    ):
        side = y_lo if low else y_hi
        values = [side[nz * k : nz * k + nz] for k in range(FACE)]
        force = []
        for a in range(3):
            rows = [jnp.broadcast_to(fc[l, a, frow : frow + 1, :], (nz, 128)) for l in range(kz)]
            v = rows[kz - 1]
            for l in range(kz - 2, -1, -1):
                v = pick(zrow < 4 * (l + 1), rows[l], v)
            force.append(v)
        there_b = jnp.broadcast_to(there, (nz, 128))
        for k, (i, v) in enumerate(beyond_face(values, list(enumerate(leave)), force, there_b)):
            o_yh[0 if low else 1, k, 0:nz, :] = v
            for to, z in enumerate((0, nz - 1)):
                post[i, to, at : at + 1, :] = v[z : z + 1]

    collide_plane(0, 0, pops, flags, fu, post)
    collide_plane(nz - 1, 1, pops, flags, fu, post)
    for side, leave, edges in ((0, leave_zm, (17, 16)), (1, leave_zp, (15, 18))):
        for k, i in enumerate(leave):
            zsc[side, ny * k : ny * k + ny, :] = post[i, side, 8 : 8 + ny, :]
        at = 5 * ny
        z = side * (nz - 1)
        for y_side, (i, rows) in enumerate(zip(edges, (y_lo, y_hi))):
            yrow = 8 + ny if y_side else 7
            zsc[side, at + y_side : at + y_side + 1, :] = post[i, side, yrow : yrow + 1, :]
            row = 9 * nz + z
            zsc[side, at + 2 + y_side : at + 3 + y_side, :] = rows[row : row + 1]
        zsc[side, at + 4 : at + 8, :] = jnp.zeros((4, 128), jnp.float32)
        zsc[side, at + 8 : at + 8 + ny, :] = flags[z].astype(jnp.float32)
    up_z = 1 - wi % 2
    o_f1[...] = zsc[up_z]
    o_f2[...] = zsc[1 - up_z]


def inner_kernel(
    pops, flags, faces, yh, fu, pot, lor, o_pops, o_near, o_pot, o_lor, obuf, post, sem_out
):
    nz, ny, nx = flags.shape
    results = [
        pltpu.make_async_copy(pot, o_pot, sem_out.at[0]),
        pltpu.make_async_copy(lor, o_lor, sem_out.at[nz - 1]),
    ]
    for c in results:
        c.start()
    for i in range(19):
        post[i, 0] = faces[i, 0]
        post[i, nz - 1] = faces[i, 1]
    for side, leave, at in ((0, leave_yp, 7), (1, leave_ym, 8 + ny)):
        for k, i in enumerate(leave):
            rows = yh[side, k]
            for z in range(1, nz - 1):
                post[i, z, at : at + 1, :] = rows[z : z + 1]

    def passing(z):
        def put(i, rows, v):
            obuf[i, z, rows, :] = v

        pass_plane(
            z,
            pops,
            flags,
            lambda i, rows: post[i, z, rows, :],
            lambda i, cz, rows: post[i, z - cz, rows, :],
            put,
        )
        pltpu.make_async_copy(obuf.at[:, z], o_pops.at[:, z], sem_out.at[z]).start()

    collide_plane(1, 1, pops, flags, fu, post)

    def plane(z, carry):
        collide_plane(z + 1, z + 1, pops, flags, fu, post)
        passing(z)
        return carry

    lax.fori_loop(1, nz - 2, plane, 0)
    passing(nz - 2)
    for i in range(19):
        o_near[i, 0] = post[i, 1]
        o_near[i, 1] = post[i, nz - 2]

    def drain(z, carry):
        pltpu.make_async_copy(obuf.at[:, z], o_pops.at[:, z], sem_out.at[z]).wait()
        return carry

    lax.fori_loop(1, nz - 1, drain, 0)
    for c in results:
        c.wait()


def outer_kernel(
    W, pops, flags, faces, near, fz1, fz2, half, o_pops, obuf, halo, sem_out
):
    nz, ny, nx = flags.shape
    wi = lax.axis_index("wide")
    even_z = wi % 2 == 0
    for side, leave, edges, there in (
        (0, leave_zp, (15, 18), wi > 0),
        (1, leave_zm, (17, 16), wi < W - 1),
    ):
        f_odd, f_even = (fz2, fz1) if side else (fz1, fz2)
        gone = jnp.broadcast_to(jnp.logical_not(there), (8, 128))
        for b in range(ny // 8):
            at = slice(5 * ny + 8 + 8 * b, 5 * ny + 16 + 8 * b)
            flag = pick(even_z, f_even[at, :], f_odd[at, :])
            shut = ((flag > 0.5) & (flag < 1.5)) | gone
            for k in range(5):
                at = slice(ny * k + 8 * b, ny * k + 8 * b + 8)
                v = pick(even_z, f_even[at, :], f_odd[at, :])
                halo[side, k, 8 + 8 * b : 16 + 8 * b, :] = pick(shut, CLOSED, v)
        at = slice(5 * ny, 5 * ny + 8)
        v = pick(even_z, f_even[at, :], f_odd[at, :])
        for y_side, i in enumerate(edges):
            flag = v[2 + y_side : 3 + y_side]
            shut = ((flag > 0.5) & (flag < 1.5)) | gone[0:1]
            yrow = 8 + ny if y_side else 7
            k = leave.index(i)
            edge = pick(shut, CLOSED, v[y_side : y_side + 1])
            halo[side, k, yrow : yrow + 1, :] = edge
    copies = []
    for side, z, leave in ((0, 0, leave_zp), (1, nz - 1, leave_zm)):

        def source(i, cz, rows, side=side, leave=leave):
            if cz == 0:
                return faces[i, side, rows, :]
            if i in leave:
                return halo[side, leave.index(i), rows, :]
            return near[i, side, rows, :]

        def put(i, rows, v, side=side):
            obuf[i, side, rows, :] = v

        pass_plane(z, pops, flags, lambda i, rows: faces[i, side, rows, :], source, put)
        copies.append(pltpu.make_async_copy(obuf.at[:, side], o_pops.at[:, z], sem_out.at[side]))
        copies[-1].start()
    for c in copies:
        c.wait()


def pair_first(size):
    return [(i, i ^ 1) for i in range(size)]


def pair_second(size, groups):
    found = []
    for g in range(groups):
        for i in range(size):
            j = i + 1 if i % 2 else i - 1
            if 0 <= j < size:
                found.append((g * size + i, g * size + j))
            elif g ^ 1 < groups:
                found.append((g * size + i, (g ^ 1) * size + i))
    return found


def solution(mesh):
    G, W, N = mesh.shape["groups"], mesh.shape["wide"], mesh.shape["narrow"]

    def per_device(populations, flags, potential, conductivity, coil_phase, phase_table, magnetic):
        f32 = jnp.float32
        nz, ny, nx = flags.shape
        kz, ky, kx = potential.shape
        yrows = y_sections(nz)[2]
        frows = 6 * ny + 8
        params = pltpu.CompilerParams(vmem_limit_bytes=VMEM_LIMIT)
        shape = jax.ShapeDtypeStruct

        def in_hbm(*xs):
            return [pltpu.with_memory_space_constraint(x, pltpu.HBM) for x in xs]

        pops_near = pltpu.with_memory_space_constraint(populations, pltpu.VMEM)
        flags_near = pltpu.with_memory_space_constraint(flags, pltpu.VMEM)
        c1, c2, own = pl.pallas_call(
            pack_coarse,
            name="pack_coarse",
            out_shape=(
                shape((2 * ky, nx), f32),
                shape((2 * ky, nx), f32),
                shape((GROUPS, 16, nx), f32),
            ),
            in_specs=[hbm_spec] * 5,
            out_specs=[vmem_spec] * 3,
            scratch_shapes=[
                pltpu.VMEM(potential.shape, f32),
                pltpu.VMEM(conductivity.shape, f32),
                pltpu.VMEM(coil_phase.shape, jnp.int32),
                pltpu.VMEM(magnetic.shape, f32),
                pltpu.SMEM(phase_table.shape, f32),
                pltpu.SemaphoreType.DMA((5,)),
            ],
            compiler_params=params,
        )(*in_hbm(potential, conductivity, coil_phase, magnetic, phase_table))
        zr1 = lax.ppermute(c1, "wide", pair_first(W))
        zr2 = lax.ppermute(c2, ("groups", "wide"), pair_second(W, G))
        fine = pl.pallas_call(
            pack_y_faces,
            name="pack_y_faces",
            out_shape=shape((2, FACE * nz, nx), f32),
            in_specs=[hbm_spec] * 2 + [any_spec],
            out_specs=vmem_spec,
            scratch_shapes=[
                pltpu.VMEM((2, 19, nz, nx), f32),
                pltpu.VMEM((2, nz, nx), jnp.int32),
                pltpu.SemaphoreType.DMA((4,)),
            ],
            compiler_params=params,
        )(*in_hbm(populations, flags), own)
        y1, y2 = pl.pallas_call(
            lambda *refs: pack_rows(ky, nz, *refs),
            name="pack_rows",
            out_shape=(shape((yrows, nx), f32), shape((yrows, nx), f32)),
            in_specs=[vmem_spec] * 4,
            out_specs=[vmem_spec] * 2,
            scratch_shapes=[pltpu.VMEM((2, yrows, nx), f32)],
            compiler_params=params,
        )(zr1, zr2, own, fine)
        yr1 = lax.ppermute(y1, "narrow", pair_first(N))
        yr2 = lax.ppermute(y2, ("groups", "narrow"), pair_second(N, G))
        pot_out, lorentz, f1, f2, faces, yh, half = pl.pallas_call(
            lambda *refs: face_kernel(W, N, *refs),
            name="faces",
            out_shape=(
                shape(potential.shape, f32),
                shape(magnetic.shape, f32),
                shape((frows, nx), f32),
                shape((frows, nx), f32),
                shape((19, 2, ny + 16, nx), f32),
                shape((2, 5, 16, nx), f32),
                shape((kz, 6, ny, nx), f32),
            ),
            in_specs=[vmem_spec] * 7,
            out_specs=[vmem_spec] * 7,
            scratch_shapes=[
                pltpu.VMEM((GROUPS + 4, 24, nx), f32),
                pltpu.VMEM((kz, 3, 24, nx), f32),
                pltpu.VMEM((2, frows, nx), f32),
            ],
            compiler_params=params,
        )(pops_near, flags_near, yr1, yr2, zr1, zr2, own)
        fz1 = lax.ppermute(f1, "wide", pair_first(W))
        fz2 = lax.ppermute(f2, ("groups", "wide"), pair_second(W, G))
        pot_near, lorentz_near = [
            pltpu.with_memory_space_constraint(x, pltpu.VMEM) for x in (pot_out, lorentz)
        ]
        inside, near, pot_out, lorentz = pl.pallas_call(
            inner_kernel,
            name="inner",
            out_shape=(
                shape(populations.shape, f32),
                shape((19, 2, ny + 16, nx), f32),
                shape(potential.shape, f32),
                shape(magnetic.shape, f32),
            ),
            in_specs=[vmem_spec] * 7,
            out_specs=[hbm_spec, vmem_spec, hbm_spec, hbm_spec],
            scratch_shapes=[
                pltpu.VMEM(populations.shape, f32),
                pltpu.VMEM((19, nz, ny + 16, nx), f32),
                pltpu.SemaphoreType.DMA((nz,)),
            ],
            compiler_params=params,
            cost_estimate=INNER_COST,
        )(pops_near, flags_near, faces, yh, half, pot_near, lorentz_near)
        passed = pl.pallas_call(
            lambda *refs: outer_kernel(W, *refs),
            name="outer",
            out_shape=shape(populations.shape, f32),
            in_specs=[vmem_spec] * 6 + [hbm_spec],
            out_specs=hbm_spec,
            input_output_aliases={6: 0},
            scratch_shapes=[
                pltpu.VMEM((19, 2, ny, nx), f32),
                pltpu.VMEM((2, 5, ny + 16, nx), f32),
                pltpu.SemaphoreType.DMA((2,)),
            ],
            compiler_params=params,
        )(pops_near, flags_near, faces, near, fz1, fz2, inside)
        return passed, pot_out, lorentz

    in_specs = (
        P(None, ("groups", "wide"), "narrow", None),
        P(("groups", "wide"), "narrow", None),
        P(("groups", "wide"), "narrow", None),
        P(("groups", "wide"), "narrow", None),
        P(("groups", "wide"), "narrow", None),
        P(),
        P(None, ("groups", "wide"), "narrow", None),
    )
    out_specs = (
        P(None, ("groups", "wide"), "narrow", None),
        P(("groups", "wide"), "narrow", None),
        P(None, ("groups", "wide"), "narrow", None),
    )
    return jax.shard_map(
        per_device, mesh=mesh, in_specs=in_specs, out_specs=out_specs, check_vma=False
    )
```

```python
import jax
import jax.numpy as jnp
from jax import lax
from jax.experimental import pallas as pl
from jax.experimental.pallas import tpu as pltpu
from jax.sharding import PartitionSpec as P

lattice_dirs = [
    (0, 0, 0),
    (1, 0, 0),
    (-1, 0, 0),
    (0, 1, 0),
    (0, -1, 0),
    (0, 0, 1),
    (0, 0, -1),
    (1, 1, 0),
    (-1, -1, 0),
    (1, -1, 0),
    (-1, 1, 0),
    (1, 0, 1),
    (-1, 0, -1),
    (1, 0, -1),
    (-1, 0, 1),
    (0, 1, 1),
    (0, -1, -1),
    (0, 1, -1),
    (0, -1, 1),
]
opposite_dir = [0, 2, 1, 4, 3, 6, 5, 8, 7, 10, 9, 12, 11, 14, 13, 16, 15, 18, 17]
pairs = [(i, opposite_dir[i]) for i in range(1, 19) if i < opposite_dir[i]]
relax_time = 0.8
force_scale = 0.02
inlet_speed = 0.05
force_factor = 1.0 - 0.5 / relax_time
PUSH = 6.0 * force_factor / 36.0

leave_yp = [3, 7, 10, 15, 17]
leave_ym = [4, 8, 9, 16, 18]
leave_zp = [5, 11, 14, 15, 18]
leave_zm = [6, 12, 13, 16, 17]

FACE = 10
GROUPS = 9
POT, SRC, COND, MX, MY, MZ, AX, AY, AZ = range(GROUPS)
RIM = 4
CLOSED = -1e30
OPEN_ABOVE = -1e29
INNER_COST = pl.CostEstimate(flops=20000000000, bytes_accessed=12000000, transcendentals=0)
TAIL = 2
VMEM_LIMIT = 24 * 1024 * 1024

any_spec = pl.BlockSpec(memory_space=pl.ANY)
hbm_spec = pl.BlockSpec(memory_space=pltpu.HBM)
vmem_spec = pl.BlockSpec(memory_space=pltpu.VMEM)


def pick(cond, a, b):
    return jnp.where(cond, a, b)


def moments(f):
    d = {}
    rho = f[0]
    for i, j in pairs:
        rho = rho + (f[i] + f[j])
        d[i] = f[i] - f[j]
    mx = d[1] + d[7] + d[9] + d[11] + d[13]
    my = d[3] + d[7] - d[9] + d[15] + d[17]
    mz = d[5] + d[11] - d[13] + d[15] - d[17]
    return rho, mx, my, mz


def coefficients(rho, inv, mom, half, push, fluid, inlet, shut):
    still = inlet | shut
    b = [pick(still, 0.0, (m + f) * inv) for m, f in zip(mom[:2], half[:2])]
    b.append(pick(still, pick(inlet, -1.5 * inlet_speed, 0.0), (mom[2] + half[2]) * inv))
    r = pick(fluid, rho * (1.0 / (36.0 * relax_time)), pick(shut, CLOSED, 1.0 / 36.0))
    p = [pick(fluid, v, 0.0) for v in push]
    r2 = r + r
    h = [r2 * v + w for v, w in zip(b, p)]
    e = [v + w for v, w in zip(h, p)]
    base = r - (b[0] * e[0] + b[1] * e[1] + b[2] * e[2]) * (1.0 / 3.0)
    keep = pick(fluid, 1.0 - 1.0 / relax_time, 0.0)
    return keep, base, b, e, h


def along(c, v):
    total = None
    for s, x in zip(c, v):
        if s == 0:
            continue
        if total is None:
            total = x if s > 0 else -x
        else:
            total = total + x if s > 0 else total - x
    return total


def post_pair(i, co):
    _, base, b, e, h = co
    c = lattice_dirs[i]
    sym = base + along(c, b) * along(c, e)
    anti = along(c, h)
    if sum(abs(s) for s in c) == 1:
        return sym + sym, anti + anti
    return sym, anti


def post_one(i, f, co):
    keep = co[0]
    if i < opposite_dir[i]:
        sym, anti = post_pair(i, co)
        return keep * f + (sym + anti)
    sym, anti = post_pair(opposite_dir[i], co)
    return keep * f + (sym - anti)


def beyond_face(values, leave, half, there):
    flag = values[9]
    shut = (flag > 0.5) & (flag < 1.5)
    shut = shut | jnp.logical_not(there)
    fluid = (flag < 0.5) & there
    inlet = (flag > 1.5) & (flag < 2.5) & there
    push = [v * PUSH for v in half]
    co = coefficients(values[5], 1.5 / values[5], values[6:9], half, push, fluid, inlet, shut)
    return [(i, post_one(i, values[k], co)) for k, i in leave]


def lanes_to(x, shift):
    shift = shift % 128
    return x if shift == 0 else pltpu.roll(x, shift, 1)


def y_sections(nz):
    found, at = [], FACE * nz
    for rows in [RIM] * 2 + [1] * (GROUPS - 2) + [RIM] * 4:
        found.append((at, rows))
        at += rows
    return found, at, at + -at % 8


def pack_coarse(
    flags,
    pot_hbm,
    cond_hbm,
    ph_hbm,
    mag_hbm,
    tab_hbm,
    o_c1,
    o_c2,
    o_g,
    fbuf,
    pot,
    cond,
    ph,
    mag,
    tab,
    sems,
):
    kz, ky, kx = pot.shape
    coarse = [
        pltpu.make_async_copy(a, b, sems.at[k])
        for k, (a, b) in enumerate(
            ((tab_hbm, tab), (ph_hbm, ph), (cond_hbm, cond), (pot_hbm, pot), (mag_hbm, mag))
        )
    ]
    nz, ny = flags.shape[0], flags.shape[1]
    up_z = 1 - lax.axis_index("wide") % 2
    copies = [
        pltpu.make_async_copy(flags.at[up_z * (nz - 1)], fbuf.at[0], sems.at[5]),
        pltpu.make_async_copy(flags.at[(1 - up_z) * (nz - 1)], fbuf.at[1], sems.at[6]),
    ]
    for c in coarse + copies:
        c.start()
    for c in coarse:
        c.wait()
    phase = ph[...]
    conductivity = cond[...]
    column = [
        pick(phase == 0, tab[0, k], pick(phase == 1, tab[1, k], tab[2, k])) for k in range(4)
    ]
    fields = [pot[...], conductivity * column[0], conductivity, mag[0], mag[1], mag[2]]
    fields += column[1:]
    blank = jnp.zeros((ky, 128 - kz * kx), jnp.float32)
    for g, field in enumerate(fields):
        row = jnp.concatenate([field[l] for l in range(kz)] + [blank], axis=1)
        o_g[g, 0:ky, :] = row
        if g <= SRC:
            o_c1[ky * g : ky * g + ky, :] = row
            o_c2[ky * g : ky * g + ky, :] = row
    for k, (c, o) in enumerate(zip(copies, (o_c1, o_c2))):
        c.wait()
        o[2 * ky : 2 * ky + ny, :] = fbuf[k].astype(jnp.float32)


def pack_y_faces(pops, flags, after, o_y, ybuf, fbuf, sems):
    nz, ny = pops.shape[1], pops.shape[2]
    copies = []
    for side, row in ((0, 0), (1, ny - 1)):
        copies.append(pltpu.make_async_copy(pops.at[:, :, row, :], ybuf.at[side], sems.at[side]))
        copies.append(pltpu.make_async_copy(flags.at[:, row, :], fbuf.at[side], sems.at[2 + side]))
    for c in copies:
        c.start()
    for c in copies:
        c.wait()
    for side, leave in ((0, leave_ym), (1, leave_yp)):
        f = [ybuf[side, i] for i in range(19)]
        values = [f[i] for i in leave] + list(moments(f))
        values.append(fbuf[side].astype(jnp.float32))
        for k, v in enumerate(values):
            o_y[side, k * nz : k * nz + nz, :] = v


def sum_cells(pops, after, mom):
    nz, ny = pops.shape[1], pops.shape[2]

    def plane(z, carry):
        for b in range(ny // 8):
            rows = slice(8 * b, 8 * b + 8)
            rho, *momenta = moments([pops[i, z, rows, :] for i in range(19)])
            for k, v in enumerate([rho, 1.5 / rho] + momenta):
                mom[k, z, rows, :] = v
        return carry

    lax.fori_loop(0, nz, plane, 0)


def coarse_blocks(ky, low, high, own):
    blocks = [own[g, 0:ky, :] for g in range(GROUPS)]
    for side in (low, high):
        blocks += [side[ky * g : ky * g + ky] for g in (POT, SRC)]
    return blocks


def pack_rows(ky, nz, zr1, zr2, own, fine, o_y1, o_y2, ysc):
    even = lax.axis_index("wide") % 2 == 0
    low = pick(even, zr2[...], zr1[...])
    high = pick(even, zr1[...], zr2[...])
    sections, used, total = y_sections(nz)
    blocks = coarse_blocks(ky, low, high, own)
    for side in range(2):
        ysc[side, 0 : FACE * nz, :] = fine[side]
        for (at, rows), v in zip(sections, blocks):
            ysc[side, at : at + rows, :] = v[ky - rows : ky] if side else v[0:rows]
        if used < total:
            ysc[side, used:total, :] = jnp.zeros((total - used, 128), jnp.float32)
    up_y = 1 - lax.axis_index("narrow") % 2
    o_y1[...] = ysc[up_y]
    o_y2[...] = ysc[1 - up_y]


def collide_plane(z, to, pops, flags, mom, fu, post):
    ny = flags.shape[1]
    l = z // 4
    for b in range(ny // 8):
        rows = slice(8 * b, 8 * b + 8)
        out = slice(8 + 8 * b, 16 + 8 * b)
        f = [pops[i, z, rows, :] for i in range(19)]
        flag = flags[z, rows, :]
        half = [fu[l, a, rows, :] for a in range(3)]
        push = [fu[l, 3 + a, rows, :] for a in range(3)]
        rho, inv, *momenta = [mom[k, z, rows, :] for k in range(5)]
        co = coefficients(rho, inv, momenta, half, push, flag == 0, flag == 2, flag == 1)
        keep = co[0]
        post[0, to, out, :] = keep * f[0] + 12.0 * co[1]
        for i, j in pairs:
            sym, anti = post_pair(i, co)
            post[i, to, out, :] = keep * f[i] + (sym + anti)
            post[j, to, out, :] = keep * f[j] + (sym - anti)


def pass_plane(z, which, pops, flags, here, source, put):
    ny, nx = flags.shape[1:]
    lane8 = lax.broadcasted_iota(jnp.int32, (8, 128), 1)
    not_first = lane8 > 0
    not_last = lane8 < nx - 1
    for b in range(ny // 8):
        rows = slice(8 * b, 8 * b + 8)
        out = slice(8 + 8 * b, 16 + 8 * b)
        wall = flags[z, rows, :] == 1
        for i in which:
            cx, cy, cz = lattice_dirs[i]
            own = here(opposite_dir[i], out)
            if i > 0:
                v = source(i, cz, slice(8 + 8 * b - cy, 16 + 8 * b - cy))
                if cx != 0:
                    v = pltpu.roll(v, cx % nx, 1)
                ok = v > OPEN_ABOVE
                if cx == 1:
                    ok = ok & not_first
                if cx == -1:
                    ok = ok & not_last
                own = pick(ok, v, own)
            put(i, rows, pick(wall, pops[i, z, rows, :], own))


def face_kernel(
    W,
    N,
    pops,
    flags,
    mom,
    yr1,
    yr2,
    zr1,
    zr2,
    own,
    o_pot,
    o_lor,
    o_f1,
    o_f2,
    post,
    o_yh,
    fu,
    ext,
    fc,
    zsc,
):
    nz, ny, nx = flags.shape
    kz, ky, kx = o_pot.shape
    wi, ni = lax.axis_index("wide"), lax.axis_index("narrow")
    even_z = wi % 2 == 0
    even_y = ni % 2 == 0
    has_low_y, has_high_y = ni > 0, ni < N - 1

    z_lo = pick(even_z, zr2[...], zr1[...])
    z_hi = pick(even_z, zr1[...], zr2[...])
    y_lo = pick(even_y, yr2[...], yr1[...])
    y_hi = pick(even_y, yr1[...], yr2[...])
    sections = y_sections(nz)[0]
    blocks = coarse_blocks(ky, z_lo, z_hi, own)
    blank = jnp.zeros((RIM, 128), jnp.float32)
    for k, ((at, rows), v) in enumerate(zip(sections, blocks)):
        if rows < RIM:
            ext[k, 0:RIM, :] = blank
            ext[k, RIM + ky : 2 * RIM + ky, :] = blank
        ext[k, RIM - rows : RIM, :] = y_lo[at : at + rows]
        ext[k, RIM : RIM + ky, :] = v
        ext[k, RIM + ky : RIM + ky + rows, :] = y_hi[at : at + rows]
        ext[k, 2 * RIM + ky : 24, :] = jnp.zeros((24 - 2 * RIM - ky, 128), jnp.float32)
    below, above = GROUPS, GROUPS + 2

    shape = (24, 128)
    lane = lax.broadcasted_iota(jnp.int32, shape, 1)
    row = lax.broadcasted_iota(jnp.int32, shape, 0)
    y_at = ni * ky + row - RIM
    y_in = (y_at >= 0) & (y_at < ky * N)
    layer = lane // kx
    x_at = lane - layer * kx

    def inside(first):
        z_at = wi * kz + first + layer
        return y_in & (z_at >= 0) & (z_at < kz * W) & (layer < kz)

    inner = [inside(-kz), inside(0), inside(kz)]

    def three(g):
        return [ext[below + g], ext[g], ext[above + g]]

    zero = jnp.zeros(shape, jnp.float32)
    field = [pick(m, v, 0.0) for m, v in zip(inner, three(POT))]
    source = three(SRC)
    last = (kz - 1) * kx

    def next_z(here, above):
        return pick(lane < last, lanes_to(here, -kx), lanes_to(above, last))

    def prev_z(here, below):
        return pick(lane >= kx, lanes_to(here, kx), lanes_to(below, -last))

    def next_x(v):
        return pick(x_at == kx - 1, 0.0, lanes_to(v, -1))

    def prev_x(v):
        return pick(x_at == 0, 0.0, lanes_to(v, 1))

    def next_y(v):
        return pltpu.roll(v, 23, 0)

    def prev_y(v):
        return pltpu.roll(v, 1, 0)

    def sweep(values, lower, upper):
        chain = [lower] + values + [upper]
        new = []
        for k in range(3):
            v = values[k]
            total = next_z(v, chain[k + 2]) + prev_z(v, chain[k])
            total = total + next_y(v) + prev_y(v)
            total = total + next_x(v) + prev_x(v)
            new.append(pick(inner[k], (total + source[k]) / 6.0, 0.0))
        return new

    field = sweep(field, zero, zero)
    field = sweep(field, zero, zero)

    v = field[1]
    grad = (
        (next_x(v) - prev_x(v)) * 0.5,
        (next_y(v) - prev_y(v)) * 0.5,
        (next_z(v, field[2]) - prev_z(v, field[0])) * 0.5,
    )
    cur = [ext[COND] * (ext[AX + a] - grad[a]) for a in range(3)]
    lorentz = [
        cur[1] * ext[MZ] - cur[2] * ext[MY],
        cur[2] * ext[MX] - cur[0] * ext[MZ],
        cur[0] * ext[MY] - cur[1] * ext[MX],
    ]
    for l in range(kz):
        o_pot[l] = lanes_to(field[1], -kx * l)[RIM : RIM + ky, 0:kx]
        for a in range(3):
            o_lor[a, l] = lanes_to(lorentz[a], -kx * l)[RIM : RIM + ky, 0:kx]

    src = lax.broadcasted_iota(jnp.int32, (128, 128), 0)
    dst = lax.broadcasted_iota(jnp.int32, (128, 128), 1) // (nx // kx)

    def widened(stack, l):
        choose = jnp.where(src == kx * l + dst, 1.0, 0.0)
        return lax.dot_general(
            stack,
            choose,
            (((1,), (0,)), ((), ())),
            precision=lax.Precision.HIGHEST,
            preferred_element_type=jnp.float32,
        )

    stack = jnp.concatenate([v * (0.5 * force_scale) for v in lorentz], axis=0)
    wide = [widened(stack, l) for l in range(kz)]
    sub = lax.broadcasted_iota(jnp.int32, (8, 128), 0)
    for l in range(kz):
        for a in range(3):
            fc[l, a] = wide[l][24 * a : 24 * a + 24]
    for l in range(kz):
        for a in range(3):
            for b in range(ny // 8):
                first = jnp.broadcast_to(fc[l, a, pl.ds(RIM + 2 * b, 1), :], (8, 128))
                second = jnp.broadcast_to(fc[l, a, pl.ds(RIM + 2 * b + 1, 1), :], (8, 128))
                half = pick(sub < 4, first, second)
                fu[l, a, 8 * b : 8 * b + 8, :] = half
                fu[l, 3 + a, 8 * b : 8 * b + 8, :] = half * PUSH

    zrow = lax.broadcasted_iota(jnp.int32, (nz, 128), 0)
    for low, leave, frow, at, there in (
        (True, leave_yp, RIM - 1, 7, has_low_y),
        (False, leave_ym, RIM + ky, 8 + ny, has_high_y),
    ):
        side = y_lo if low else y_hi
        values = [side[nz * k : nz * k + nz] for k in range(FACE)]
        force = []
        for a in range(3):
            rows = [jnp.broadcast_to(fc[l, a, frow : frow + 1, :], (nz, 128)) for l in range(kz)]
            v = rows[kz - 1]
            for l in range(kz - 2, -1, -1):
                v = pick(zrow < 4 * (l + 1), rows[l], v)
            force.append(v)
        there_b = jnp.broadcast_to(there, (nz, 128))
        for k, (i, v) in enumerate(beyond_face(values, list(enumerate(leave)), force, there_b)):
            o_yh[0 if low else 1, k, 0:nz, :] = v
            for to, z in enumerate((0, nz - 1)):
                post[i, to, at : at + 1, :] = v[z : z + 1]

    collide_plane(0, 0, pops, flags, mom, fu, post)
    collide_plane(nz - 1, 1, pops, flags, mom, fu, post)
    for side, leave, edges in ((0, leave_zm, (17, 16)), (1, leave_zp, (15, 18))):
        for k, i in enumerate(leave):
            zsc[side, ny * k : ny * k + ny, :] = post[i, side, 8 : 8 + ny, :]
        at = 5 * ny
        z = side * (nz - 1)
        for y_side, (i, rows) in enumerate(zip(edges, (y_lo, y_hi))):
            yrow = 8 + ny if y_side else 7
            zsc[side, at + y_side : at + y_side + 1, :] = post[i, side, yrow : yrow + 1, :]
            row = 9 * nz + z
            zsc[side, at + 2 + y_side : at + 3 + y_side, :] = rows[row : row + 1]
        zsc[side, at + 4 : at + 8, :] = jnp.zeros((4, 128), jnp.float32)
    up_z = 1 - wi % 2
    o_f1[...] = zsc[up_z]
    o_f2[...] = zsc[1 - up_z]


def runs(which):
    found = []
    for i in which:
        if found and found[-1][0] + found[-1][1] == i:
            found[-1] = (found[-1][0], found[-1][1] + 1)
        else:
            found.append((i, 1))
    return found


staying_low = [i for i in range(19) if i not in leave_zp]
staying_high = [i for i in range(19) if i not in leave_zm]


def inner_kernel(
    pops,
    flags,
    mom,
    faces,
    yh,
    fu,
    pot,
    lor,
    o_pops,
    o_tail,
    o_pot,
    o_lor,
    obuf,
    post,
    sem_out,
    sem_edge,
    sem_coarse,
):
    nz, ny, nx = flags.shape
    results = [
        pltpu.make_async_copy(pot, o_pot, sem_coarse.at[0]),
        pltpu.make_async_copy(lor, o_lor, sem_coarse.at[1]),
    ]
    for c in results:
        c.start()
    for side, leave, at in ((0, leave_yp, 7), (1, leave_ym, 8 + ny)):
        for k, i in enumerate(leave):
            rows = yh[side, k]
            for z in range(1, nz - 1):
                post[i, z, at : at + 1, :] = rows[z : z + 1]

    def read(i, z, rows):
        if isinstance(z, int) and z in (0, nz - 1):
            return faces[i, 0 if z == 0 else 1, rows, :]
        return post[i, z, rows, :]

    def passing(z, which, into, at):
        def put(i, rows, v):
            into[i, at, rows, :] = v

        pass_plane(
            z,
            which,
            pops,
            flags,
            lambda i, rows: read(i, z, rows),
            lambda i, cz, rows: read(i, z - cz, rows),
            put,
        )

    def edge(z, which, sem):
        passing(z, which, obuf, z)
        for k, (first, length) in enumerate(runs(which)):
            part = pl.ds(first, length)
            c = pltpu.make_async_copy(obuf.at[part, z], o_pops.at[part, z], sem_edge.at[sem, k])
            c.start()
            results.append(c)

    def out(z):
        passing(z, range(19), obuf, z)
        pltpu.make_async_copy(obuf.at[:, z], o_pops.at[:, z], sem_out.at[z]).start()

    collide_plane(1, 1, pops, flags, mom, fu, post)
    edge(0, staying_low, 0)
    collide_plane(nz - 2, nz - 2, pops, flags, mom, fu, post)
    edge(nz - 1, staying_high, 1)
    collide_plane(2, 2, pops, flags, mom, fu, post)
    out(1)
    last = nz - 1 - TAIL

    def plane(z, carry):
        collide_plane(z + 1, z + 1, pops, flags, mom, fu, post)
        out(z)
        return carry

    lax.fori_loop(2, last, plane, 0)
    for z in range(last + 1, nz - 2):
        collide_plane(z, z, pops, flags, mom, fu, post)
    for k in range(TAIL):
        passing(last + k, range(19), o_tail, k)

    def drain(z, carry):
        pltpu.make_async_copy(obuf.at[:, z], o_pops.at[:, z], sem_out.at[z]).wait()
        return carry

    lax.fori_loop(1, last, drain, 0)
    for c in results:
        c.wait()


def outer_kernel(
    W, ky, pops, flags, faces, tail, fz1, fz2, zr1, zr2, half, o_pops, obuf, halo, sems, sem_tail
):
    nz, ny, nx = flags.shape
    wi = lax.axis_index("wide")
    even_z = wi % 2 == 0
    copies = [
        pltpu.make_async_copy(tail.at[:, k], o_pops.at[:, nz - 1 - TAIL + k], sem_tail.at[k])
        for k in range(TAIL)
    ]
    for c in copies:
        c.start()
    for side, leave, edges, there in (
        (0, leave_zp, (15, 18), wi > 0),
        (1, leave_zm, (17, 16), wi < W - 1),
    ):
        f_odd, f_even = (fz2, fz1) if side else (fz1, fz2)
        c_odd, c_even = (zr2, zr1) if side else (zr1, zr2)
        gone = jnp.broadcast_to(jnp.logical_not(there), (8, 128))
        for b in range(ny // 8):
            at = slice(2 * ky + 8 * b, 2 * ky + 8 * b + 8)
            flag = pick(even_z, c_even[at, :], c_odd[at, :])
            shut = ((flag > 0.5) & (flag < 1.5)) | gone
            for k in range(5):
                at = slice(ny * k + 8 * b, ny * k + 8 * b + 8)
                v = pick(even_z, f_even[at, :], f_odd[at, :])
                halo[side, k, 8 + 8 * b : 16 + 8 * b, :] = pick(shut, CLOSED, v)
        at = slice(5 * ny, 5 * ny + 8)
        v = pick(even_z, f_even[at, :], f_odd[at, :])
        for y_side, i in enumerate(edges):
            flag = v[2 + y_side : 3 + y_side]
            shut = ((flag > 0.5) & (flag < 1.5)) | gone[0:1]
            yrow = 8 + ny if y_side else 7
            k = leave.index(i)
            edge = pick(shut, CLOSED, v[y_side : y_side + 1])
            halo[side, k, yrow : yrow + 1, :] = edge
    for side, z, leave in ((0, 0, leave_zp), (1, nz - 1, leave_zm)):

        def source(i, cz, rows, side=side, leave=leave):
            return halo[side, leave.index(i), rows, :]

        def put(i, rows, v, side=side):
            obuf[side, i, rows, :] = v

        pass_plane(
            z, leave, pops, flags, lambda i, rows: faces[i, side, rows, :], source, put
        )
        for k, (first, length) in enumerate(runs(leave)):
            part = pl.ds(first, length)
            c = pltpu.make_async_copy(obuf.at[side, part], o_pops.at[part, z], sems.at[side, k])
            c.start()
            copies.append(c)
    for c in copies:
        c.wait()


def pair_first(size):
    return [(i, i ^ 1) for i in range(size)]


def pair_second(size, groups):
    found = []
    for g in range(groups):
        for i in range(size):
            j = i + 1 if i % 2 else i - 1
            if 0 <= j < size:
                found.append((g * size + i, g * size + j))
            elif g ^ 1 < groups:
                found.append((g * size + i, (g ^ 1) * size + i))
    return found


def solution(mesh):
    G, W, N = mesh.shape["groups"], mesh.shape["wide"], mesh.shape["narrow"]

    def per_device(populations, flags, potential, conductivity, coil_phase, phase_table, magnetic):
        f32 = jnp.float32
        nz, ny, nx = flags.shape
        kz, ky, kx = potential.shape
        yrows = y_sections(nz)[2]
        frows = 5 * ny + 8
        params = pltpu.CompilerParams(vmem_limit_bytes=VMEM_LIMIT)
        shape = jax.ShapeDtypeStruct

        def in_hbm(*xs):
            return [pltpu.with_memory_space_constraint(x, pltpu.HBM) for x in xs]

        pops_near = pltpu.with_memory_space_constraint(populations, pltpu.VMEM)
        flags_near = pltpu.with_memory_space_constraint(flags, pltpu.VMEM)
        c1, c2, own = pl.pallas_call(
            pack_coarse,
            name="pack_coarse",
            out_shape=(
                shape((2 * ky + ny, nx), f32),
                shape((2 * ky + ny, nx), f32),
                shape((GROUPS, 16, nx), f32),
            ),
            in_specs=[hbm_spec] * 6,
            out_specs=[vmem_spec] * 3,
            scratch_shapes=[
                pltpu.VMEM((2, ny, nx), jnp.int32),
                pltpu.VMEM(potential.shape, f32),
                pltpu.VMEM(conductivity.shape, f32),
                pltpu.VMEM(coil_phase.shape, jnp.int32),
                pltpu.VMEM(magnetic.shape, f32),
                pltpu.SMEM(phase_table.shape, f32),
                pltpu.SemaphoreType.DMA((7,)),
            ],
            compiler_params=params,
        )(*in_hbm(flags, potential, conductivity, coil_phase, magnetic, phase_table))
        zr1 = lax.ppermute(c1, "wide", pair_first(W))
        zr2 = lax.ppermute(c2, ("groups", "wide"), pair_second(W, G))
        fine = pl.pallas_call(
            pack_y_faces,
            name="pack_y_faces",
            out_shape=shape((2, FACE * nz, nx), f32),
            in_specs=[hbm_spec] * 2 + [any_spec],
            out_specs=vmem_spec,
            scratch_shapes=[
                pltpu.VMEM((2, 19, nz, nx), f32),
                pltpu.VMEM((2, nz, nx), jnp.int32),
                pltpu.SemaphoreType.DMA((4,)),
            ],
            compiler_params=params,
        )(*in_hbm(populations, flags), own)
        y1, y2 = pl.pallas_call(
            lambda *refs: pack_rows(ky, nz, *refs),
            name="pack_rows",
            out_shape=(shape((yrows, nx), f32), shape((yrows, nx), f32)),
            in_specs=[vmem_spec] * 4,
            out_specs=[vmem_spec] * 2,
            scratch_shapes=[pltpu.VMEM((2, yrows, nx), f32)],
            compiler_params=params,
        )(zr1, zr2, own, fine)
        yr1 = lax.ppermute(y1, "narrow", pair_first(N))
        yr2 = lax.ppermute(y2, ("groups", "narrow"), pair_second(N, G))
        mom = pl.pallas_call(
            sum_cells,
            name="sum_cells",
            out_shape=shape((5, nz, ny, nx), f32),
            in_specs=[vmem_spec, any_spec],
            out_specs=vmem_spec,
            compiler_params=params,
        )(pops_near, y1)
        pot_out, lorentz, f1, f2, faces, yh, half = pl.pallas_call(
            lambda *refs: face_kernel(W, N, *refs),
            name="faces",
            out_shape=(
                shape(potential.shape, f32),
                shape(magnetic.shape, f32),
                shape((frows, nx), f32),
                shape((frows, nx), f32),
                shape((19, 2, ny + 16, nx), f32),
                shape((2, 5, 16, nx), f32),
                shape((kz, 6, ny, nx), f32),
            ),
            in_specs=[vmem_spec] * 8,
            out_specs=[vmem_spec] * 7,
            scratch_shapes=[
                pltpu.VMEM((GROUPS + 4, 24, nx), f32),
                pltpu.VMEM((kz, 3, 24, nx), f32),
                pltpu.VMEM((2, frows, nx), f32),
            ],
            compiler_params=params,
        )(pops_near, flags_near, mom, yr1, yr2, zr1, zr2, own)
        fz1 = lax.ppermute(f1, "wide", pair_first(W))
        fz2 = lax.ppermute(f2, ("groups", "wide"), pair_second(W, G))
        pot_near, lorentz_near = [
            pltpu.with_memory_space_constraint(x, pltpu.VMEM) for x in (pot_out, lorentz)
        ]
        inside, tail, pot_out, lorentz = pl.pallas_call(
            inner_kernel,
            name="inner",
            out_shape=(
                shape(populations.shape, f32),
                shape((19, TAIL, ny, nx), f32),
                shape(potential.shape, f32),
                shape(magnetic.shape, f32),
            ),
            in_specs=[vmem_spec] * 8,
            out_specs=[hbm_spec, vmem_spec, hbm_spec, hbm_spec],
            scratch_shapes=[
                pltpu.VMEM(populations.shape, f32),
                pltpu.VMEM((19, nz, ny + 16, nx), f32),
                pltpu.SemaphoreType.DMA((nz,)),
                pltpu.SemaphoreType.DMA((2, 4)),
                pltpu.SemaphoreType.DMA((2,)),
            ],
            compiler_params=params,
            cost_estimate=INNER_COST,
        )(pops_near, flags_near, mom, faces, yh, half, pot_near, lorentz_near)
        passed = pl.pallas_call(
            lambda *refs: outer_kernel(W, ky, *refs),
            name="outer",
            out_shape=shape(populations.shape, f32),
            in_specs=[vmem_spec] * 8 + [hbm_spec],
            out_specs=hbm_spec,
            input_output_aliases={8: 0},
            scratch_shapes=[
                pltpu.VMEM((2, 19, ny, nx), f32),
                pltpu.VMEM((2, 5, ny + 16, nx), f32),
                pltpu.SemaphoreType.DMA((2, 4)),
                pltpu.SemaphoreType.DMA((TAIL,)),
            ],
            compiler_params=params,
        )(pops_near, flags_near, faces, tail, fz1, fz2, zr1, zr2, inside)
        return passed, pot_out, lorentz

    in_specs = (
        P(None, ("groups", "wide"), "narrow", None),
        P(("groups", "wide"), "narrow", None),
        P(("groups", "wide"), "narrow", None),
        P(("groups", "wide"), "narrow", None),
        P(("groups", "wide"), "narrow", None),
        P(),
        P(None, ("groups", "wide"), "narrow", None),
    )
    out_specs = (
        P(None, ("groups", "wide"), "narrow", None),
        P(("groups", "wide"), "narrow", None),
        P(None, ("groups", "wide"), "narrow", None),
    )
    return jax.shard_map(
        per_device, mesh=mesh, in_specs=in_specs, out_specs=out_specs, check_vma=False
    )
```

```python
import jax
import jax.numpy as jnp
from jax import lax
from jax.experimental import pallas as pl
from jax.experimental.pallas import tpu as pltpu
from jax.sharding import PartitionSpec as P

lattice_dirs = [
    (0, 0, 0),
    (1, 0, 0),
    (-1, 0, 0),
    (0, 1, 0),
    (0, -1, 0),
    (0, 0, 1),
    (0, 0, -1),
    (1, 1, 0),
    (-1, -1, 0),
    (1, -1, 0),
    (-1, 1, 0),
    (1, 0, 1),
    (-1, 0, -1),
    (1, 0, -1),
    (-1, 0, 1),
    (0, 1, 1),
    (0, -1, -1),
    (0, 1, -1),
    (0, -1, 1),
]
opposite_dir = [0, 2, 1, 4, 3, 6, 5, 8, 7, 10, 9, 12, 11, 14, 13, 16, 15, 18, 17]
pairs = [(i, opposite_dir[i]) for i in range(1, 19) if i < opposite_dir[i]]
relax_time = 0.8
force_scale = 0.02
inlet_speed = 0.05
force_factor = 1.0 - 0.5 / relax_time
PUSH = 6.0 * force_factor / 36.0

leave_yp = [3, 7, 10, 15, 17]
leave_ym = [4, 8, 9, 16, 18]
leave_zp = [5, 11, 14, 15, 18]
leave_zm = [6, 12, 13, 16, 17]

FACE = 10
GROUPS = 9
POT, SRC, COND, MX, MY, MZ, AX, AY, AZ = range(GROUPS)
RIM = 4
CLOSED = -1e30
OPEN_ABOVE = -1e29
INNER_COST = pl.CostEstimate(flops=20000000000, bytes_accessed=12000000, transcendentals=0)
TAIL = 2
VMEM_LIMIT = 24 * 1024 * 1024

any_spec = pl.BlockSpec(memory_space=pl.ANY)
hbm_spec = pl.BlockSpec(memory_space=pltpu.HBM)
vmem_spec = pl.BlockSpec(memory_space=pltpu.VMEM)


def pick(cond, a, b):
    return jnp.where(cond, a, b)


def moments(f):
    d = {}
    rho = f[0]
    for i, j in pairs:
        rho = rho + (f[i] + f[j])
        d[i] = f[i] - f[j]
    mx = d[1] + d[7] + d[9] + d[11] + d[13]
    my = d[3] + d[7] - d[9] + d[15] + d[17]
    mz = d[5] + d[11] - d[13] + d[15] - d[17]
    return rho, mx, my, mz


def coefficients(rho, inv, mom, half, push, fluid, inlet, shut):
    still = inlet | shut
    b = [pick(still, 0.0, (m + f) * inv) for m, f in zip(mom[:2], half[:2])]
    b.append(pick(still, pick(inlet, -1.5 * inlet_speed, 0.0), (mom[2] + half[2]) * inv))
    r = pick(fluid, rho * (1.0 / (36.0 * relax_time)), pick(shut, CLOSED, 1.0 / 36.0))
    p = [pick(fluid, v, 0.0) for v in push]
    r2 = r + r
    h = [r2 * v + w for v, w in zip(b, p)]
    e = [v + w for v, w in zip(h, p)]
    base = r - (b[0] * e[0] + b[1] * e[1] + b[2] * e[2]) * (1.0 / 3.0)
    keep = pick(fluid, 1.0 - 1.0 / relax_time, 0.0)
    return keep, base, b, e, h


def along(c, v):
    total = None
    for s, x in zip(c, v):
        if s == 0:
            continue
        if total is None:
            total = x if s > 0 else -x
        else:
            total = total + x if s > 0 else total - x
    return total


def post_pair(i, co):
    _, base, b, e, h = co
    c = lattice_dirs[i]
    sym = base + along(c, b) * along(c, e)
    anti = along(c, h)
    if sum(abs(s) for s in c) == 1:
        return sym + sym, anti + anti
    return sym, anti


def post_one(i, f, co):
    keep = co[0]
    if i < opposite_dir[i]:
        sym, anti = post_pair(i, co)
        return keep * f + (sym + anti)
    sym, anti = post_pair(opposite_dir[i], co)
    return keep * f + (sym - anti)


def beyond_face(values, leave, half, there):
    flag = values[9]
    shut = (flag > 0.5) & (flag < 1.5)
    shut = shut | jnp.logical_not(there)
    fluid = (flag < 0.5) & there
    inlet = (flag > 1.5) & (flag < 2.5) & there
    push = [v * PUSH for v in half]
    co = coefficients(values[5], 1.5 / values[5], values[6:9], half, push, fluid, inlet, shut)
    return [(i, post_one(i, values[k], co)) for k, i in leave]


def lanes_to(x, shift):
    shift = shift % 128
    return x if shift == 0 else pltpu.roll(x, shift, 1)


def y_sections(nz):
    found, at = [], FACE * nz
    for rows in [RIM] * 2 + [1] * (GROUPS - 2) + [RIM] * 4:
        found.append((at, rows))
        at += rows
    return found, at, at + -at % 8


def pack_coarse(
    flags,
    pot_hbm,
    cond_hbm,
    ph_hbm,
    mag_hbm,
    tab_hbm,
    o_c1,
    o_c2,
    o_g,
    fbuf,
    pot,
    cond,
    ph,
    mag,
    tab,
    sems,
):
    kz, ky, kx = pot.shape
    coarse = [
        pltpu.make_async_copy(a, b, sems.at[k])
        for k, (a, b) in enumerate(
            ((tab_hbm, tab), (ph_hbm, ph), (cond_hbm, cond), (pot_hbm, pot), (mag_hbm, mag))
        )
    ]
    nz, ny = flags.shape[0], flags.shape[1]
    up_z = 1 - lax.axis_index("wide") % 2
    copies = [
        pltpu.make_async_copy(flags.at[up_z * (nz - 1)], fbuf.at[0], sems.at[5]),
        pltpu.make_async_copy(flags.at[(1 - up_z) * (nz - 1)], fbuf.at[1], sems.at[6]),
    ]
    for c in coarse + copies:
        c.start()
    for c in coarse:
        c.wait()
    phase = ph[...]
    conductivity = cond[...]
    column = [
        pick(phase == 0, tab[0, k], pick(phase == 1, tab[1, k], tab[2, k])) for k in range(4)
    ]
    fields = [pot[...], conductivity * column[0], conductivity, mag[0], mag[1], mag[2]]
    fields += column[1:]
    blank = jnp.zeros((ky, 128 - kz * kx), jnp.float32)
    for g, field in enumerate(fields):
        row = jnp.concatenate([field[l] for l in range(kz)] + [blank], axis=1)
        o_g[g, 0:ky, :] = row
        if g <= SRC:
            o_c1[ky * g : ky * g + ky, :] = row
            o_c2[ky * g : ky * g + ky, :] = row
    for k, (c, o) in enumerate(zip(copies, (o_c1, o_c2))):
        c.wait()
        o[2 * ky : 2 * ky + ny, :] = fbuf[k].astype(jnp.float32)


def pack_y_faces(pops, flags, after, o_y, ybuf, fbuf, sems):
    nz, ny = pops.shape[1], pops.shape[2]
    copies = []
    for side, row in ((0, 0), (1, ny - 1)):
        copies.append(pltpu.make_async_copy(pops.at[:, :, row, :], ybuf.at[side], sems.at[side]))
        copies.append(pltpu.make_async_copy(flags.at[:, row, :], fbuf.at[side], sems.at[2 + side]))
    for c in copies:
        c.start()
    for c in copies:
        c.wait()
    for side, leave in ((0, leave_ym), (1, leave_yp)):
        f = [ybuf[side, i] for i in range(19)]
        values = [f[i] for i in leave] + list(moments(f))
        values.append(fbuf[side].astype(jnp.float32))
        for k, v in enumerate(values):
            o_y[side, k * nz : k * nz + nz, :] = v


def sum_cells(pops, after, mom):
    nz, ny = pops.shape[1], pops.shape[2]

    def plane(z, carry):
        for b in range(ny // 8):
            rows = slice(8 * b, 8 * b + 8)
            rho, *momenta = moments([pops[i, z, rows, :] for i in range(19)])
            for k, v in enumerate([rho, 1.5 / rho] + momenta):
                mom[k, z, rows, :] = v
        return carry

    lax.fori_loop(0, nz, plane, 0)


def coarse_blocks(ky, low, high, own):
    blocks = [own[g, 0:ky, :] for g in range(GROUPS)]
    for side in (low, high):
        blocks += [side[ky * g : ky * g + ky] for g in (POT, SRC)]
    return blocks


def pack_rows(ky, nz, zr1, zr2, own, fine, o_y1, o_y2, ysc):
    even = lax.axis_index("wide") % 2 == 0
    low = pick(even, zr2[...], zr1[...])
    high = pick(even, zr1[...], zr2[...])
    sections, used, total = y_sections(nz)
    blocks = coarse_blocks(ky, low, high, own)
    for side in range(2):
        ysc[side, 0 : FACE * nz, :] = fine[side]
        for (at, rows), v in zip(sections, blocks):
            ysc[side, at : at + rows, :] = v[ky - rows : ky] if side else v[0:rows]
        if used < total:
            ysc[side, used:total, :] = jnp.zeros((total - used, 128), jnp.float32)
    up_y = 1 - lax.axis_index("narrow") % 2
    o_y1[...] = ysc[up_y]
    o_y2[...] = ysc[1 - up_y]


def collide_plane(z, to, pops, flags, mom, fu, post):
    ny = flags.shape[1]
    l = z // 4
    for b in range(ny // 8):
        rows = slice(8 * b, 8 * b + 8)
        out = slice(8 + 8 * b, 16 + 8 * b)
        f = [pops[i, z, rows, :] for i in range(19)]
        flag = flags[z, rows, :]
        half = [fu[l, a, rows, :] for a in range(3)]
        push = [fu[l, 3 + a, rows, :] for a in range(3)]
        rho, inv, *momenta = [mom[k, z, rows, :] for k in range(5)]
        co = coefficients(rho, inv, momenta, half, push, flag == 0, flag == 2, flag == 1)
        keep = co[0]
        post[0, to, out, :] = keep * f[0] + 12.0 * co[1]
        for i, j in pairs:
            sym, anti = post_pair(i, co)
            post[i, to, out, :] = keep * f[i] + (sym + anti)
            post[j, to, out, :] = keep * f[j] + (sym - anti)


def pass_plane(z, which, pops, flags, here, source, put):
    ny, nx = flags.shape[1:]
    lane8 = lax.broadcasted_iota(jnp.int32, (8, 128), 1)
    not_first = lane8 > 0
    not_last = lane8 < nx - 1
    for b in range(ny // 8):
        rows = slice(8 * b, 8 * b + 8)
        out = slice(8 + 8 * b, 16 + 8 * b)
        wall = flags[z, rows, :] == 1
        for i in which:
            cx, cy, cz = lattice_dirs[i]
            own = here(opposite_dir[i], out)
            if i > 0:
                v = source(i, cz, slice(8 + 8 * b - cy, 16 + 8 * b - cy))
                if cx != 0:
                    v = pltpu.roll(v, cx % nx, 1)
                ok = v > OPEN_ABOVE
                if cx == 1:
                    ok = ok & not_first
                if cx == -1:
                    ok = ok & not_last
                own = pick(ok, v, own)
            put(i, rows, pick(wall, pops[i, z, rows, :], own))


def face_kernel(
    W,
    N,
    pops,
    flags,
    mom,
    yr1,
    yr2,
    zr1,
    zr2,
    own,
    o_pot,
    o_lor,
    o_f1,
    o_f2,
    post,
    o_yh,
    fu,
    ext,
    fc,
    zsc,
):
    nz, ny, nx = flags.shape
    kz, ky, kx = o_pot.shape
    wi, ni = lax.axis_index("wide"), lax.axis_index("narrow")
    even_z = wi % 2 == 0
    even_y = ni % 2 == 0
    has_low_y, has_high_y = ni > 0, ni < N - 1

    z_lo = pick(even_z, zr2[...], zr1[...])
    z_hi = pick(even_z, zr1[...], zr2[...])
    y_lo = pick(even_y, yr2[...], yr1[...])
    y_hi = pick(even_y, yr1[...], yr2[...])
    sections = y_sections(nz)[0]
    blocks = coarse_blocks(ky, z_lo, z_hi, own)
    blank = jnp.zeros((RIM, 128), jnp.float32)
    for k, ((at, rows), v) in enumerate(zip(sections, blocks)):
        if rows < RIM:
            ext[k, 0:RIM, :] = blank
            ext[k, RIM + ky : 2 * RIM + ky, :] = blank
        ext[k, RIM - rows : RIM, :] = y_lo[at : at + rows]
        ext[k, RIM : RIM + ky, :] = v
        ext[k, RIM + ky : RIM + ky + rows, :] = y_hi[at : at + rows]
        ext[k, 2 * RIM + ky : 24, :] = jnp.zeros((24 - 2 * RIM - ky, 128), jnp.float32)
    below, above = GROUPS, GROUPS + 2

    shape = (24, 128)
    lane = lax.broadcasted_iota(jnp.int32, shape, 1)
    row = lax.broadcasted_iota(jnp.int32, shape, 0)
    y_at = ni * ky + row - RIM
    y_in = (y_at >= 0) & (y_at < ky * N)
    layer = lane // kx
    x_at = lane - layer * kx

    def inside(first):
        z_at = wi * kz + first + layer
        return y_in & (z_at >= 0) & (z_at < kz * W) & (layer < kz)

    inner = [inside(-kz), inside(0), inside(kz)]

    def three(g):
        return [ext[below + g], ext[g], ext[above + g]]

    zero = jnp.zeros(shape, jnp.float32)
    field = [pick(m, v, 0.0) for m, v in zip(inner, three(POT))]
    source = three(SRC)
    last = (kz - 1) * kx

    def next_z(here, above):
        return pick(lane < last, lanes_to(here, -kx), lanes_to(above, last))

    def prev_z(here, below):
        return pick(lane >= kx, lanes_to(here, kx), lanes_to(below, -last))

    def next_x(v):
        return pick(x_at == kx - 1, 0.0, lanes_to(v, -1))

    def prev_x(v):
        return pick(x_at == 0, 0.0, lanes_to(v, 1))

    def next_y(v):
        return pltpu.roll(v, 23, 0)

    def prev_y(v):
        return pltpu.roll(v, 1, 0)

    def sweep(values, lower, upper):
        chain = [lower] + values + [upper]
        new = []
        for k in range(3):
            v = values[k]
            total = next_z(v, chain[k + 2]) + prev_z(v, chain[k])
            total = total + next_y(v) + prev_y(v)
            total = total + next_x(v) + prev_x(v)
            new.append(pick(inner[k], (total + source[k]) / 6.0, 0.0))
        return new

    field = sweep(field, zero, zero)
    field = sweep(field, zero, zero)

    v = field[1]
    grad = (
        (next_x(v) - prev_x(v)) * 0.5,
        (next_y(v) - prev_y(v)) * 0.5,
        (next_z(v, field[2]) - prev_z(v, field[0])) * 0.5,
    )
    cur = [ext[COND] * (ext[AX + a] - grad[a]) for a in range(3)]
    lorentz = [
        cur[1] * ext[MZ] - cur[2] * ext[MY],
        cur[2] * ext[MX] - cur[0] * ext[MZ],
        cur[0] * ext[MY] - cur[1] * ext[MX],
    ]
    for l in range(kz):
        o_pot[l] = lanes_to(field[1], -kx * l)[RIM : RIM + ky, 0:kx]
        for a in range(3):
            o_lor[a, l] = lanes_to(lorentz[a], -kx * l)[RIM : RIM + ky, 0:kx]

    src = lax.broadcasted_iota(jnp.int32, (128, 128), 0)
    dst = lax.broadcasted_iota(jnp.int32, (128, 128), 1) // (nx // kx)

    def widened(stack, l):
        choose = jnp.where(src == kx * l + dst, 1.0, 0.0)
        return lax.dot_general(
            stack,
            choose,
            (((1,), (0,)), ((), ())),
            precision=lax.Precision.HIGHEST,
            preferred_element_type=jnp.float32,
        )

    stack = jnp.concatenate([v * (0.5 * force_scale) for v in lorentz], axis=0)
    wide = [widened(stack, l) for l in range(kz)]
    sub = lax.broadcasted_iota(jnp.int32, (8, 128), 0)
    for l in range(kz):
        for a in range(3):
            fc[l, a] = wide[l][24 * a : 24 * a + 24]
    for l in range(kz):
        for a in range(3):
            for b in range(ny // 8):
                first = jnp.broadcast_to(fc[l, a, pl.ds(RIM + 2 * b, 1), :], (8, 128))
                second = jnp.broadcast_to(fc[l, a, pl.ds(RIM + 2 * b + 1, 1), :], (8, 128))
                half = pick(sub < 4, first, second)
                fu[l, a, 8 * b : 8 * b + 8, :] = half
                fu[l, 3 + a, 8 * b : 8 * b + 8, :] = half * PUSH

    zrow = lax.broadcasted_iota(jnp.int32, (nz, 128), 0)
    for low, leave, frow, at, there in (
        (True, leave_yp, RIM - 1, 7, has_low_y),
        (False, leave_ym, RIM + ky, 8 + ny, has_high_y),
    ):
        side = y_lo if low else y_hi
        values = [side[nz * k : nz * k + nz] for k in range(FACE)]
        force = []
        for a in range(3):
            rows = [jnp.broadcast_to(fc[l, a, frow : frow + 1, :], (nz, 128)) for l in range(kz)]
            v = rows[kz - 1]
            for l in range(kz - 2, -1, -1):
                v = pick(zrow < 4 * (l + 1), rows[l], v)
            force.append(v)
        there_b = jnp.broadcast_to(there, (nz, 128))
        for k, (i, v) in enumerate(beyond_face(values, list(enumerate(leave)), force, there_b)):
            o_yh[0 if low else 1, k, 0:nz, :] = v
            for to, z in enumerate((0, nz - 1)):
                post[i, to, at : at + 1, :] = v[z : z + 1]

    collide_plane(0, 0, pops, flags, mom, fu, post)
    collide_plane(nz - 1, 1, pops, flags, mom, fu, post)
    for side, leave, edges in ((0, leave_zm, (17, 16)), (1, leave_zp, (15, 18))):
        for k, i in enumerate(leave):
            zsc[side, ny * k : ny * k + ny, :] = post[i, side, 8 : 8 + ny, :]
        at = 5 * ny
        z = side * (nz - 1)
        for y_side, (i, rows) in enumerate(zip(edges, (y_lo, y_hi))):
            yrow = 8 + ny if y_side else 7
            zsc[side, at + y_side : at + y_side + 1, :] = post[i, side, yrow : yrow + 1, :]
            row = 9 * nz + z
            zsc[side, at + 2 + y_side : at + 3 + y_side, :] = rows[row : row + 1]
        zsc[side, at + 4 : at + 8, :] = jnp.zeros((4, 128), jnp.float32)
    up_z = 1 - wi % 2
    o_f1[...] = zsc[up_z]
    o_f2[...] = zsc[1 - up_z]


def runs(which):
    found = []
    for i in which:
        if found and found[-1][0] + found[-1][1] == i:
            found[-1] = (found[-1][0], found[-1][1] + 1)
        else:
            found.append((i, 1))
    return found


staying_low = [i for i in range(19) if i not in leave_zp]
staying_high = [i for i in range(19) if i not in leave_zm]


def inner_kernel(
    pops,
    flags,
    mom,
    faces,
    yh,
    fu,
    pot,
    lor,
    o_pops,
    o_tail,
    o_pot,
    o_lor,
    obuf,
    post,
    sem_out,
    sem_edge,
    sem_coarse,
):
    nz, ny, nx = flags.shape
    results = [
        pltpu.make_async_copy(pot, o_pot, sem_coarse.at[0]),
        pltpu.make_async_copy(lor, o_lor, sem_coarse.at[1]),
    ]
    for c in results:
        c.start()
    for side, leave, at in ((0, leave_yp, 7), (1, leave_ym, 8 + ny)):
        for k, i in enumerate(leave):
            rows = yh[side, k]
            for z in range(1, nz - 1):
                post[i, z, at : at + 1, :] = rows[z : z + 1]

    def read(i, z, rows):
        if isinstance(z, int) and z in (0, nz - 1):
            return faces[i, 0 if z == 0 else 1, rows, :]
        return post[i, z, rows, :]

    def passing(z, which, into, at):
        def put(i, rows, v):
            into[i, at, rows, :] = v

        pass_plane(
            z,
            which,
            pops,
            flags,
            lambda i, rows: read(i, z, rows),
            lambda i, cz, rows: read(i, z - cz, rows),
            put,
        )

    def edge(z, which, sem):
        passing(z, which, obuf, z)
        for k, (first, length) in enumerate(runs(which)):
            part = pl.ds(first, length)
            c = pltpu.make_async_copy(obuf.at[part, z], o_pops.at[part, z], sem_edge.at[sem, k])
            c.start()
            results.append(c)

    def out(z):
        passing(z, range(19), obuf, z)
        pltpu.make_async_copy(obuf.at[:, z], o_pops.at[:, z], sem_out.at[z]).start()

    collide_plane(1, 1, pops, flags, mom, fu, post)
    edge(0, staying_low, 0)
    collide_plane(nz - 2, nz - 2, pops, flags, mom, fu, post)
    edge(nz - 1, staying_high, 1)
    collide_plane(2, 2, pops, flags, mom, fu, post)
    out(1)
    last = nz - 1 - TAIL

    def plane(z, carry):
        collide_plane(z + 1, z + 1, pops, flags, mom, fu, post)
        out(z)
        return carry

    lax.fori_loop(2, last, plane, 0)
    for z in range(last + 1, nz - 2):
        collide_plane(z, z, pops, flags, mom, fu, post)
    for k in range(TAIL):
        passing(last + k, range(19), o_tail, k)

    def drain(z, carry):
        pltpu.make_async_copy(obuf.at[:, z], o_pops.at[:, z], sem_out.at[z]).wait()
        return carry

    lax.fori_loop(1, last, drain, 0)
    for c in results:
        c.wait()


def outer_kernel(
    W, ky, pops, flags, faces, tail, fz1, fz2, zr1, zr2, half, o_pops, obuf, halo, sems, sem_tail
):
    nz, ny, nx = flags.shape
    wi = lax.axis_index("wide")
    even_z = wi % 2 == 0
    copies = [
        pltpu.make_async_copy(tail.at[:, k], o_pops.at[:, nz - 1 - TAIL + k], sem_tail.at[k])
        for k in range(TAIL)
    ]
    for c in copies:
        c.start()
    for side, leave, edges, there in (
        (0, leave_zp, (15, 18), wi > 0),
        (1, leave_zm, (17, 16), wi < W - 1),
    ):
        f_odd, f_even = (fz2, fz1) if side else (fz1, fz2)
        c_odd, c_even = (zr2, zr1) if side else (zr1, zr2)
        gone = jnp.broadcast_to(jnp.logical_not(there), (8, 128))
        for b in range(ny // 8):
            at = slice(2 * ky + 8 * b, 2 * ky + 8 * b + 8)
            flag = pick(even_z, c_even[at, :], c_odd[at, :])
            shut = ((flag > 0.5) & (flag < 1.5)) | gone
            for k in range(5):
                at = slice(ny * k + 8 * b, ny * k + 8 * b + 8)
                v = pick(even_z, f_even[at, :], f_odd[at, :])
                halo[side, k, 8 + 8 * b : 16 + 8 * b, :] = pick(shut, CLOSED, v)
        at = slice(5 * ny, 5 * ny + 8)
        v = pick(even_z, f_even[at, :], f_odd[at, :])
        for y_side, i in enumerate(edges):
            flag = v[2 + y_side : 3 + y_side]
            shut = ((flag > 0.5) & (flag < 1.5)) | gone[0:1]
            yrow = 8 + ny if y_side else 7
            k = leave.index(i)
            edge = pick(shut, CLOSED, v[y_side : y_side + 1])
            halo[side, k, yrow : yrow + 1, :] = edge
    for side, z, leave in ((0, 0, leave_zp), (1, nz - 1, leave_zm)):

        def source(i, cz, rows, side=side, leave=leave):
            return halo[side, leave.index(i), rows, :]

        def put(i, rows, v, side=side):
            obuf[side, i, rows, :] = v

        pass_plane(
            z, leave, pops, flags, lambda i, rows: faces[i, side, rows, :], source, put
        )
        for k, (first, length) in enumerate(runs(leave)):
            part = pl.ds(first, length)
            c = pltpu.make_async_copy(obuf.at[side, part], o_pops.at[part, z], sems.at[side, k])
            c.start()
            copies.append(c)
    for c in copies:
        c.wait()


def pair_first(size):
    return [(i, i ^ 1) for i in range(size)]


def pair_second(size, other, major):
    def at(i, k):
        return k * size + i if major else i * other + k

    found = []
    for k in range(other):
        for i in range(size):
            j = i + 1 if i % 2 else i - 1
            if 0 <= j < size:
                found.append((at(i, k), at(j, k)))
            elif k ^ 1 < other:
                found.append((at(i, k), at(i, k ^ 1)))
    return found


def solution(mesh):
    G, W, N = mesh.shape["groups"], mesh.shape["wide"], mesh.shape["narrow"]

    def per_device(populations, flags, potential, conductivity, coil_phase, phase_table, magnetic):
        f32 = jnp.float32
        nz, ny, nx = flags.shape
        kz, ky, kx = potential.shape
        yrows = y_sections(nz)[2]
        frows = 5 * ny + 8
        params = pltpu.CompilerParams(vmem_limit_bytes=VMEM_LIMIT)
        shape = jax.ShapeDtypeStruct

        def in_hbm(*xs):
            return [pltpu.with_memory_space_constraint(x, pltpu.HBM) for x in xs]

        pops_near = pltpu.with_memory_space_constraint(populations, pltpu.VMEM)
        flags_near = pltpu.with_memory_space_constraint(flags, pltpu.VMEM)
        c1, c2, own = pl.pallas_call(
            pack_coarse,
            name="pack_coarse",
            out_shape=(
                shape((2 * ky + ny, nx), f32),
                shape((2 * ky + ny, nx), f32),
                shape((GROUPS, 16, nx), f32),
            ),
            in_specs=[hbm_spec] * 6,
            out_specs=[vmem_spec] * 3,
            scratch_shapes=[
                pltpu.VMEM((2, ny, nx), jnp.int32),
                pltpu.VMEM(potential.shape, f32),
                pltpu.VMEM(conductivity.shape, f32),
                pltpu.VMEM(coil_phase.shape, jnp.int32),
                pltpu.VMEM(magnetic.shape, f32),
                pltpu.SMEM(phase_table.shape, f32),
                pltpu.SemaphoreType.DMA((7,)),
            ],
            compiler_params=params,
        )(*in_hbm(flags, potential, conductivity, coil_phase, magnetic, phase_table))
        zr1 = lax.ppermute(c1, "wide", pair_first(W))
        zr2 = lax.ppermute(c2, ("wide", "narrow"), pair_second(W, N, False))
        fine = pl.pallas_call(
            pack_y_faces,
            name="pack_y_faces",
            out_shape=shape((2, FACE * nz, nx), f32),
            in_specs=[hbm_spec] * 2 + [any_spec],
            out_specs=vmem_spec,
            scratch_shapes=[
                pltpu.VMEM((2, 19, nz, nx), f32),
                pltpu.VMEM((2, nz, nx), jnp.int32),
                pltpu.SemaphoreType.DMA((4,)),
            ],
            compiler_params=params,
        )(*in_hbm(populations, flags), own)
        y1, y2 = pl.pallas_call(
            lambda *refs: pack_rows(ky, nz, *refs),
            name="pack_rows",
            out_shape=(shape((yrows, nx), f32), shape((yrows, nx), f32)),
            in_specs=[vmem_spec] * 4,
            out_specs=[vmem_spec] * 2,
            scratch_shapes=[pltpu.VMEM((2, yrows, nx), f32)],
            compiler_params=params,
        )(zr1, zr2, own, fine)
        yr1 = lax.ppermute(y1, "narrow", pair_first(N))
        yr2 = lax.ppermute(y2, ("groups", "narrow"), pair_second(N, G, True))
        mom = pl.pallas_call(
            sum_cells,
            name="sum_cells",
            out_shape=shape((5, nz, ny, nx), f32),
            in_specs=[vmem_spec, any_spec],
            out_specs=vmem_spec,
            compiler_params=params,
        )(pops_near, y1)
        pot_out, lorentz, f1, f2, faces, yh, half = pl.pallas_call(
            lambda *refs: face_kernel(W, N, *refs),
            name="faces",
            out_shape=(
                shape(potential.shape, f32),
                shape(magnetic.shape, f32),
                shape((frows, nx), f32),
                shape((frows, nx), f32),
                shape((19, 2, ny + 16, nx), f32),
                shape((2, 5, 16, nx), f32),
                shape((kz, 6, ny, nx), f32),
            ),
            in_specs=[vmem_spec] * 8,
            out_specs=[vmem_spec] * 7,
            scratch_shapes=[
                pltpu.VMEM((GROUPS + 4, 24, nx), f32),
                pltpu.VMEM((kz, 3, 24, nx), f32),
                pltpu.VMEM((2, frows, nx), f32),
            ],
            compiler_params=params,
        )(pops_near, flags_near, mom, yr1, yr2, zr1, zr2, own)
        fz1 = lax.ppermute(f1, "wide", pair_first(W))
        fz2 = lax.ppermute(f2, ("wide", "narrow"), pair_second(W, N, False))
        pot_near, lorentz_near = [
            pltpu.with_memory_space_constraint(x, pltpu.VMEM) for x in (pot_out, lorentz)
        ]
        inside, tail, pot_out, lorentz = pl.pallas_call(
            inner_kernel,
            name="inner",
            out_shape=(
                shape(populations.shape, f32),
                shape((19, TAIL, ny, nx), f32),
                shape(potential.shape, f32),
                shape(magnetic.shape, f32),
            ),
            in_specs=[vmem_spec] * 8,
            out_specs=[hbm_spec, vmem_spec, hbm_spec, hbm_spec],
            scratch_shapes=[
                pltpu.VMEM(populations.shape, f32),
                pltpu.VMEM((19, nz, ny + 16, nx), f32),
                pltpu.SemaphoreType.DMA((nz,)),
                pltpu.SemaphoreType.DMA((2, 4)),
                pltpu.SemaphoreType.DMA((2,)),
            ],
            compiler_params=params,
            cost_estimate=INNER_COST,
        )(pops_near, flags_near, mom, faces, yh, half, pot_near, lorentz_near)
        passed = pl.pallas_call(
            lambda *refs: outer_kernel(W, ky, *refs),
            name="outer",
            out_shape=shape(populations.shape, f32),
            in_specs=[vmem_spec] * 8 + [hbm_spec],
            out_specs=hbm_spec,
            input_output_aliases={8: 0},
            scratch_shapes=[
                pltpu.VMEM((2, 19, ny, nx), f32),
                pltpu.VMEM((2, 5, ny + 16, nx), f32),
                pltpu.SemaphoreType.DMA((2, 4)),
                pltpu.SemaphoreType.DMA((TAIL,)),
            ],
            compiler_params=params,
        )(pops_near, flags_near, faces, tail, fz1, fz2, zr1, zr2, inside)
        return passed, pot_out, lorentz

    in_specs = (
        P(None, ("groups", "wide"), "narrow", None),
        P(("groups", "wide"), "narrow", None),
        P(("groups", "wide"), "narrow", None),
        P(("groups", "wide"), "narrow", None),
        P(("groups", "wide"), "narrow", None),
        P(),
        P(None, ("groups", "wide"), "narrow", None),
    )
    out_specs = (
        P(None, ("groups", "wide"), "narrow", None),
        P(("groups", "wide"), "narrow", None),
        P(None, ("groups", "wide"), "narrow", None),
    )
    return jax.shard_map(
        per_device, mesh=mesh, in_specs=in_specs, out_specs=out_specs, check_vma=False
    )
```
